128 devices in a mesh: dp: 4 (over x), gz: 32 (over y, z, core).
Axes of the slice: x: 4, y: 4, z: 4, core: 2. Of those that a mesh axis runs over, the one named last changes fastest.
Arguments:
- fields: bfloat16 [4, 256, 16, 128, 128], P('dp', 'gz'), may hold values from -6 to 6
- cotangent: bfloat16 [4, 256, 16, 128, 128], P('dp', 'gz'), may hold values from -6 to 6
- spectral_weight: bfloat16 [2, 16, 16, 32768], P(None, None, None, 'gz'), may hold values from -1.5 to 1.5
- pointwise_weight: bfloat16 [16, 16], replicated, may hold values from -1.5 to 1.5
Outputs:
- layer_output: bfloat16 [4, 256, 16, 128, 128], P('dp', 'gz')
- input_grad: bfloat16 [4, 256, 16, 128, 128], P('dp', 'gz')
- pointwise_grad: float32 [16, 16], replicated
- spectral_grad: float32 [2, 16, 16, 32768], P(None, None, None, 'gz')
The draws below stay inside these ranges and needn't reach their ends.
All inputs are finite; a program needn't handle non-finite values.
Results may differ from the reference program's by a relative error of at most 0.001.
Values sent between devices are 32-bit elements; how exact they have to be, the bound alone decides.
A program may use at most 128 MiB of HBM per device.

```python
import math
import jax
import jax.numpy as jnp
from jax import lax

C = 16
M = 32
X = 128
Y = 128
Z = 256
SAMPLES = 4
MODES = 32768


def level_of(stream_key, dims, pieces, smallest, high):
    def one(position, blocks):
        steps = jax.random.uniform(jax.random.fold_in(jax.random.fold_in(stream_key, 6), position), (blocks,), jnp.float32, smallest / len(pieces), high / len(pieces))
        return jnp.repeat(jnp.exp(steps), dims[position] // blocks).reshape((-1,) + (1,) * (len(dims) - position - 1))

    loudness = one(*pieces[0])
    for cut in pieces[1:]:
        loudness = loudness * one(*cut)
    return loudness


def bell_draw(own_key, dims, width, reach, shards=(), kind=jnp.bfloat16):
    gain = level_of(own_key, dims, shards, -0.22, 0.18) if shards else 1.0
    drawn = jax.random.normal(own_key, dims, jnp.float32) * width * gain
    return jnp.minimum(jnp.maximum(drawn, -reach), reach).astype(kind)


def setup_inputs(seed: int = 0) -> dict:
    keys = jax.random.split(jax.random.key(seed), 5)
    return {
        "fields": bell_draw(keys[0], (SAMPLES, Z, C, X, Y), 1.0, 6.0, ((0, 4), (1, 32))),
        "cotangent": bell_draw(keys[1], (SAMPLES, Z, C, X, Y), 1.0, 6.0, ((0, 4), (1, 32))),
        "spectral_weight": bell_draw(keys[2], (2, C, C, MODES), C ** -0.5, 1.5, ((3, 32),)),
        "pointwise_weight": bell_draw(keys[3], (C, C), C ** -0.5, 1.5),
    }


HIGHEST = lax.Precision.HIGHEST

def angle_table(length, modes, first, count):
    positions = first + jnp.arange(count, dtype=jnp.int32)
    frequency = jnp.arange(modes, dtype=jnp.int32)
    phase = positions[:, None] * frequency[None, :] % length
    angles = phase.astype(jnp.float32) * (2.0 * math.pi / length)
    return (jnp.cos(angles), jnp.sin(angles))

def plane_forward(field, cos_x, sin_x, cos_y, sin_y):
    modes = cos_x.shape[1]
    section = jnp.einsum('szcxy,yb->szcxb', field, jnp.concatenate([cos_y, -sin_y], axis=1), precision=HIGHEST)
    block = jnp.einsum('szcxb,xa->szcab', section, jnp.concatenate([cos_x, -sin_x], axis=1), precision=HIGHEST)
    real_part = block[..., :modes, :modes] - block[..., modes:, modes:]
    imag_part = block[..., :modes, modes:] + block[..., modes:, :modes]
    shape = real_part.shape[:3] + (modes * modes,)
    return jnp.stack([real_part.reshape(shape), imag_part.reshape(shape)])

def depth_forward(planes, cos_z, sin_z):

    def contract(values, table):
        return jnp.einsum('szcp,zk->scpk', values, table, precision=HIGHEST)
    real_out = contract(planes[0], cos_z) + contract(planes[1], sin_z)
    imag_out = contract(planes[1], cos_z) - contract(planes[0], sin_z)
    shape = real_out.shape[:2] + (real_out.shape[2] * real_out.shape[3],)
    return jnp.stack([real_out.reshape(shape), imag_out.reshape(shape)])

def depth_inverse(spectrum, cos_z, sin_z):
    modes = cos_z.shape[1]
    shape = spectrum.shape[1:3] + (spectrum.shape[3] // modes, modes)
    real_in = spectrum[0].reshape(shape)
    imag_in = spectrum[1].reshape(shape)

    def expand(values, table):
        return jnp.einsum('scpk,zk->szcp', values, table, precision=HIGHEST)
    real_out = expand(real_in, cos_z) - expand(imag_in, sin_z)
    imag_out = expand(real_in, sin_z) + expand(imag_in, cos_z)
    return jnp.stack([real_out, imag_out])

def plane_inverse(planes, cos_x, sin_x, cos_y, sin_y):
    modes = cos_x.shape[1]
    shape = planes.shape[1:4] + (modes, modes)
    real_in = planes[0].reshape(shape)
    imag_in = planes[1].reshape(shape)

    def spread(values, table):
        return jnp.einsum('szcab,xa->szcxb', values, table, precision=HIGHEST)
    real_mid = spread(real_in, cos_x) - spread(imag_in, sin_x)
    imag_mid = spread(real_in, sin_x) + spread(imag_in, cos_x)
    joined = jnp.concatenate([real_mid, imag_mid], axis=-1)
    return jnp.einsum('szcxb,yb->szcxy', joined, jnp.concatenate([cos_y, -sin_y], axis=1), precision=HIGHEST)

def mix_modes(spectrum, weight):

    def term(values, table):
        return jnp.einsum('scm,com->som', values, table, precision=HIGHEST)
    real_out = term(spectrum[0], weight[0]) - term(spectrum[1], weight[1])
    imag_out = term(spectrum[0], weight[1]) + term(spectrum[1], weight[0])
    return jnp.stack([real_out, imag_out])

def mix_adjoint(grad_spec, weight):

    def term(values, table):
        return jnp.einsum('som,com->scm', values, table, precision=HIGHEST)
    real_out = term(grad_spec[0], weight[0]) + term(grad_spec[1], weight[1])
    imag_out = term(grad_spec[1], weight[0]) - term(grad_spec[0], weight[1])
    return jnp.stack([real_out, imag_out])

def mix_weight_grad(spectrum, grad_spec):

    def term(values, other):
        return jnp.einsum('scm,som->com', values, other, precision=HIGHEST)
    real_out = term(spectrum[0], grad_spec[0]) + term(spectrum[1], grad_spec[1])
    imag_out = term(spectrum[0], grad_spec[1]) - term(spectrum[1], grad_spec[0])
    return jnp.stack([real_out, imag_out])

def gelu_tanh(values):
    return jax.nn.gelu(values, approximate=True)

def reference(fields, cotangent, spectral_weight, pointwise_weight):
    cos_x, sin_x = angle_table(X, M, 0, X)
    cos_y, sin_y = angle_table(Y, M, 0, Y)
    cos_z, sin_z = angle_table(Z, M, 0, Z)
    scale = 1.0 / math.sqrt(X * Y * Z * MODES)
    weight = spectral_weight.astype(jnp.float32)
    mixing = pointwise_weight.astype(jnp.float32)

    def one_sample(pair):
        field, cot = pair
        inputs = field.astype(jnp.float32)[None]
        input_spec = depth_forward(plane_forward(inputs, cos_x, sin_x, cos_y, sin_y), cos_z, sin_z)
        mixed = mix_modes(input_spec, weight)
        spectral = plane_inverse(depth_inverse(mixed, cos_z, sin_z), cos_x, sin_x, cos_y, sin_y) * scale
        pointwise = jnp.einsum('szcxy,co->szoxy', inputs, mixing, precision=HIGHEST)
        pre = spectral + pointwise
        activation, pullback = jax.vjp(gelu_tanh, pre)
        grad_pre = pullback(cot.astype(jnp.float32)[None])[0]
        grad_spec = depth_forward(plane_forward(grad_pre, cos_x, sin_x, cos_y, sin_y), cos_z, sin_z) * scale
        adjoint = mix_adjoint(grad_spec, weight)
        back = plane_inverse(depth_inverse(adjoint, cos_z, sin_z), cos_x, sin_x, cos_y, sin_y)
        grad_input = back + jnp.einsum('szoxy,co->szcxy', grad_pre, mixing, precision=HIGHEST)
        point_term = jnp.einsum('szcxy,szoxy->co', inputs, grad_pre, precision=HIGHEST)
        spec_term = mix_weight_grad(input_spec, grad_spec)
        return (activation[0].astype(jnp.bfloat16), grad_input[0].astype(jnp.bfloat16), point_term, spec_term)
    outputs = lax.map(one_sample, (fields, cotangent))
    cells = SAMPLES * X * Y * Z
    pointwise_grad = lax.optimization_barrier(jnp.sum(outputs[2], axis=0)) * (1.0 / math.sqrt(cells))
    spectral_grad = lax.optimization_barrier(jnp.sum(outputs[3], axis=0)) * math.sqrt(MODES / cells)
    return (outputs[0], outputs[1], pointwise_grad, spectral_grad)
```

```python
import math

import jax
import jax.numpy as jnp
import ml_dtypes
import numpy as np
from jax import lax
from jax.experimental import pallas as pl
from jax.experimental.pallas import tpu as pltpu
from jax.sharding import PartitionSpec as P

M = 32
C = 16
ZL = 8
X = 128
Y = 128
Z = 256
GROUPS = 32
SAMPLES = 4
MODES = M * M * M
CELLS = SAMPLES * X * Y * Z
SCALE = 1.0 / math.sqrt(X * Y * Z * MODES)
BF = jnp.bfloat16
F32 = jnp.float32
VMEM_LIMIT = 60 * 1024 * 1024
K0 = math.sqrt(2.0 / math.pi)
K1 = K0 * 0.044715


def halves(table):
    high = table.astype(ml_dtypes.bfloat16)
    low = (table - high.astype(np.float64)).astype(ml_dtypes.bfloat16)
    return high, low


def wave(length, left, right):
    phase = np.outer(left, right) % length
    angle = phase * (2.0 * np.pi / length)
    return np.cos(angle), np.sin(angle)


def make_tables():
    modes = np.arange(M)
    ky = 4 * (modes % 8) + modes // 8
    tables = {}
    cos_x, sin_x = wave(X, modes, np.arange(X))
    high, low = halves(np.concatenate([cos_x, -sin_x]))
    zero = np.zeros_like(low)
    tables["xf"] = np.concatenate([high, low])
    tables["xg"] = np.concatenate(
        [np.concatenate([high, high], 1), np.concatenate([low, zero], 1)]
    )
    for name, scale in (("xi", SCALE), ("xj", 1.0)):
        high, low = halves(scale * np.concatenate([cos_x, -sin_x]).T)
        tables[name] = np.concatenate([high, high, low], 1)
    cos_y, sin_y = wave(Y, np.arange(Y), ky)
    forward = np.zeros((4, 2, Y, 2, 4, M))
    inverse = np.zeros((4, 2, 4, M, 2, Y))
    for k in range(4):
        forward[k, 0, :, 0, k] = cos_y
        forward[k, 1, :, 0, k] = sin_y
        forward[k, 0, :, 1, k] = -sin_y
        forward[k, 1, :, 1, k] = cos_y
        inverse[k, 0, k, :, 0] = cos_y.T
        inverse[k, 1, k, :, 0] = -sin_y.T
        inverse[k, 0, k, :, 1] = sin_y.T
        inverse[k, 1, k, :, 1] = cos_y.T
    tables["yf"] = np.stack(halves(forward.reshape(1024, 256)))
    tables["yi"] = np.stack(halves(inverse.reshape(1024, 256)))
    cos_z, sin_z = wave(Z, np.arange(Z), np.tile(modes, 4))
    tables["zf"] = np.stack(
        halves(
            np.concatenate(
                [np.concatenate([cos_z, -sin_z], 1), np.concatenate([sin_z, cos_z], 1)]
            )
        )
    )
    tables["zi"] = np.stack(halves(np.concatenate([cos_z, sin_z], 1)))
    return tables


TABLES = make_tables()


def dot(a, b):
    return lax.dot_general(a, b, (((1,), (0,)), ((), ())), preferred_element_type=F32)


def dot_nt(a, b):
    return lax.dot_general(a, b, (((1,), (1,)), ((), ())), preferred_element_type=F32)


def split(values):
    high = values.astype(BF)
    return high, (values - high.astype(F32)).astype(BF)


def rows_of_plane(section, lhs_high, lhs_low, first, k):
    for zz in range(2):
        lanes = slice(zz * Y, (zz + 1) * Y)
        row = jnp.concatenate([section[:M, lanes], section[M:, lanes]], axis=1)
        high, low = split(row)
        at = (slice((first + zz) * M, (first + zz + 1) * M), slice(k * 256, (k + 1) * 256))
        lhs_high[at] = high
        lhs_low[at] = low


def finish_forward(lhs_high, lhs_low, yf, out):
    high = lhs_high[...]
    total = dot(high, yf[0]) + dot(lhs_low[...], yf[0]) + dot(high, yf[1])
    flat = out.reshape(512, 128)
    for z in range(ZL):
        for part in range(2):
            flat[pl.ds(part * ZL + z, M, stride=16), :] = total[
                z * M : (z + 1) * M, part * 128 : (part + 1) * 128
            ]


def field_kernel(field, xf, yf, out, lhs_high, lhs_low):
    for zp in range(ZL // 2):
        for k in range(4):
            pair = jnp.concatenate([field[0, 2 * zp, k], field[0, 2 * zp + 1, k]], axis=1)
            both = dot(xf[...], pair)
            rows_of_plane(both[:64] + both[64:], lhs_high, lhs_low, 2 * zp, k)
    finish_forward(lhs_high, lhs_low, yf, out)


def depth_forward(planes, zf, rows):
    for group in range(4):
        for part in range(2):
            turned = planes[:, group, part * ZL : (part + 1) * ZL, :].reshape(Z, 128).T
            for k in range(4):
                for j in range(4):
                    rows[
                        j * 128 + (group * 4 + k) * 8 : j * 128 + (group * 4 + k + 1) * 8,
                        part * 256 : (part + 1) * 256,
                    ] = turned[k * 32 + j * 8 : k * 32 + j * 8 + 8]
    high, low = split(rows[...])
    wide = dot(high, zf[0]) + dot(low, zf[0]) + dot(high, zf[1])
    which = lax.broadcasted_iota(jnp.int32, (128, 256), 1) // 32 % 4
    total = wide[:128]
    for j in range(1, 4):
        total = jnp.where(which == j, wide[j * 128 : (j + 1) * 128], total)
    return total


def depth_inverse(spectrum, zi, out):
    lane = lax.broadcasted_iota(jnp.int32, (8, 128), 1) // 32
    for group in range(4):
        blocks = []
        for part in range(2):
            pieces = []
            for k in range(4):
                at = (group * 4 + k) * 8
                tile = spectrum[part, at : at + 8, :]
                pieces += [jnp.where(lane == j, tile, 0.0) for j in range(4)]
            blocks.append(jnp.concatenate(pieces, axis=0))
        real_in, imag_in = blocks
        right = jnp.concatenate(
            [
                jnp.concatenate([real_in, -imag_in], axis=1),
                jnp.concatenate([imag_in, real_in], axis=1),
            ],
            axis=0,
        )
        high, low = split(right)
        total = dot_nt(zi[0], high) + dot_nt(zi[0], low) + dot_nt(zi[1], high)
        for part in range(2):
            out[:, group, part * ZL : (part + 1) * ZL, :] = total[
                :, part * 128 : (part + 1) * 128
            ].reshape(GROUPS, ZL, 128)


def mix_kernel(planes, weight, zf, zi, spec_out, out, rows, mixed):
    spec = depth_forward(planes, zf, rows)
    spec_out[0] = spec[:, :128]
    spec_out[1] = spec[:, 128:]
    for g in range(8):
        lanes = slice(g * 128, (g + 1) * 128)
        real_out = jnp.zeros((C, 128), F32)
        imag_out = jnp.zeros((C, 128), F32)
        for c in range(C):
            real_in = spec_out[0, c * 8 + g : c * 8 + g + 1, :]
            imag_in = spec_out[1, c * 8 + g : c * 8 + g + 1, :]
            wr = weight[0, c, :, lanes].astype(F32)
            wi = weight[1, c, :, lanes].astype(F32)
            real_out += real_in * wr - imag_in * wi
            imag_out += real_in * wi + imag_in * wr
        mixed[0, pl.ds(g, C, stride=8), :] = real_out
        mixed[1, pl.ds(g, C, stride=8), :] = imag_out
    depth_inverse(mixed, zi, out)


def adjoint_kernel(planes, weight, zf, zi, spec_out, out, rows, mixed):
    spec = depth_forward(planes, zf, rows) * SCALE
    spec_out[0] = spec[:, :128]
    spec_out[1] = spec[:, 128:]
    for g in range(8):
        lanes = slice(g * 128, (g + 1) * 128)
        real_in = spec_out[0, pl.ds(g, C, stride=8), :]
        imag_in = spec_out[1, pl.ds(g, C, stride=8), :]
        for c in range(C):
            wr = weight[0, c, :, lanes].astype(F32)
            wi = weight[1, c, :, lanes].astype(F32)
            at = slice(c * 8 + g, c * 8 + g + 1)
            mixed[0, at, :] = jnp.sum(real_in * wr + imag_in * wi, axis=0, keepdims=True)
            mixed[1, at, :] = jnp.sum(imag_in * wr - real_in * wi, axis=0, keepdims=True)
    depth_inverse(mixed, zi, out)


def weight_grad_kernel(spec, grad, out):
    factor = math.sqrt(MODES / CELLS)
    for g in range(8):
        lanes = slice(g * 128, (g + 1) * 128)
        grads = [
            (
                grad[s, 0, pl.ds(g, C, stride=8), :] * factor,
                grad[s, 1, pl.ds(g, C, stride=8), :] * factor,
            )
            for s in range(SAMPLES)
        ]
        for c in range(C):
            real_out = jnp.zeros((C, 128), F32)
            imag_out = jnp.zeros((C, 128), F32)
            for s in range(SAMPLES):
                ur = spec[s, 0, c * 8 + g : c * 8 + g + 1, :]
                ui = spec[s, 1, c * 8 + g : c * 8 + g + 1, :]
                gr, gi = grads[s]
                real_out += ur * gr + ui * gi
                imag_out += ur * gi - ui * gr
            out[0, c, :, lanes] = real_out
            out[1, c, :, lanes] = imag_out


def plane_inverse(planes, yi, xi, store):
    flat = planes.reshape(512, 128)
    parts = [
        jnp.concatenate(
            [flat[pl.ds(part * ZL + z, M, stride=16), :] for part in range(2)], axis=1
        )
        for z in range(ZL)
    ]
    high, low = split(jnp.concatenate(parts, axis=0))
    for k in range(4):
        right = yi[0, k * 256 : (k + 1) * 256, :]
        middle = dot(high, right) + dot(low, right) + dot(high, yi[1, k * 256 : (k + 1) * 256, :])
        for zp in range(ZL // 2):
            first = middle[(2 * zp) * M : (2 * zp + 1) * M]
            second = middle[(2 * zp + 1) * M : (2 * zp + 2) * M]
            stacked = jnp.concatenate(
                [
                    jnp.concatenate([first[:, :Y], second[:, :Y]], axis=1),
                    jnp.concatenate([first[:, Y:], second[:, Y:]], axis=1),
                ],
                axis=0,
            )
            up, down = split(stacked)
            both = dot(xi[...], jnp.concatenate([up, down, up], axis=0))
            store(2 * zp, k, both[:, :Y])
            store(2 * zp + 1, k, both[:, Y:])


def cells_of(ref, zp, xb):
    pair = [
        ref[0, 2 * zp + zz, :, pl.ds(pl.multiple_of(xb * 16, 16), 16), :].reshape(C * 16, Y)
        for zz in range(2)
    ]
    return jnp.concatenate(pair, axis=1)


def output_kernel(
    planes, field, cot, pw, yi, xi, xg, yf,
    act_out, high_out, low_out, grad_planes, point_out,
    pre, lhs_high, lhs_low, point,
):
    def store(z, k, plane):
        pre[z, k] = plane

    plane_inverse(planes, yi, xi, store)
    point[...] = jnp.zeros_like(point)

    @pl.loop(0, X // 16)
    def _(xb):
        rows = pl.ds(pl.multiple_of(xb * 16, 16), 16)
        total = None
        for zp in range(ZL // 2):
            cells = cells_of(field, zp, xb)
            local = dot(pw[...], cells)
            grads = []
            for zz in range(2):
                z = 2 * zp + zz
                values = pre[z, :, rows, :].reshape(64, Y) + local[:, zz * Y : (zz + 1) * Y]
                square = values * values
                half = 0.5 + 0.5 * jnp.tanh(values * (K0 + K1 * square))
                act = values * half
                slope = half + values * (2.0 * K0 + 6.0 * K1 * square) * (half - half * half)
                grad = cot[0, z, :, rows, :].reshape(64, Y).astype(F32) * slope
                high, low = split(grad)
                act_out[0, z, :, rows, :] = act.astype(BF).reshape(4, 16, Y)
                high_out[0, z, :, rows, :] = high.reshape(4, 16, Y)
                low_out[0, z, :, rows, :] = low.reshape(4, 16, Y)
                grads.append(jnp.concatenate([high, low], axis=0))
            term = dot_nt(jnp.concatenate(grads, axis=1), cells)
            total = term if total is None else total + term
        point[...] += total

    both = point[0:64] + point[64:128]
    row = lax.broadcasted_iota(jnp.int32, (16, 256), 0)
    lane = lax.broadcasted_iota(jnp.int32, (16, 256), 1) % 16
    for k in range(4):
        kept = jnp.where(row == lane, both[k * 16 : (k + 1) * 16], 0.0)
        point_out[0, k : k + 1, :] = jnp.sum(kept, axis=0, keepdims=True)

    for zp in range(ZL // 2):
        for k in range(4):
            stacked = jnp.concatenate(
                [
                    jnp.concatenate([ref[0, 2 * zp, k], ref[0, 2 * zp + 1, k]], axis=1)
                    for ref in (high_out, low_out)
                ],
                axis=0,
            )
            both = dot(xg[...], stacked)
            rows_of_plane(both[:64] + both[64:], lhs_high, lhs_low, 2 * zp, k)
    finish_forward(lhs_high, lhs_low, yf, grad_planes)


def input_kernel(planes, high_in, low_in, pw, yi, xj, out, pre):
    def store(z, k, plane):
        pre[z, k] = plane

    plane_inverse(planes, yi, xj, store)

    @pl.loop(0, X // 16)
    def _(xb):
        rows = pl.ds(pl.multiple_of(xb * 16, 16), 16)
        for zp in range(ZL // 2):
            local = dot(pw[...], cells_of(high_in, zp, xb)) + dot(
                pw[...], cells_of(low_in, zp, xb)
            )
            for zz in range(2):
                z = 2 * zp + zz
                values = pre[z, :, rows, :].reshape(64, Y) + local[:, zz * Y : (zz + 1) * Y]
                out[0, z, :, rows, :] = values.astype(BF).reshape(4, 16, Y)


def whole(shape):
    return pl.BlockSpec(shape, lambda i: (0,) * len(shape))


GRID_BLOCK = pl.BlockSpec((1, ZL, 4, X, Y), lambda i: (0, 0, i, 0, 0))
GRID_FULL = whole((1, ZL, C, X, Y))
LANE_BLOCK = pl.BlockSpec((GROUPS, 1, 16, 128), lambda i: (0, i, 0, 0))
GRID_SHAPE = jax.ShapeDtypeStruct((1, ZL, C, X, Y), BF)
PLANES_SHAPE = jax.ShapeDtypeStruct((GROUPS, 4, 16, 128), F32)
SPEC_SHAPE = jax.ShapeDtypeStruct((2, 128, 128), F32)


def params():
    return pltpu.CompilerParams(vmem_limit_bytes=VMEM_LIMIT)


def table(name):
    return jnp.asarray(TABLES[name])


def field_forward(fields):
    return pl.pallas_call(
        field_kernel,
        grid=(4,),
        in_specs=[GRID_BLOCK, whole((128, 128)), whole((2, 1024, 256))],
        out_specs=LANE_BLOCK,
        out_shape=PLANES_SHAPE,
        scratch_shapes=[pltpu.VMEM((256, 1024), BF)] * 2,
        compiler_params=params(),
        name="field_forward",
    )(fields, table("xf"), table("yf"))


def mode_call(kernel, name, planes, weight):
    return pl.pallas_call(
        kernel,
        out_shape=(SPEC_SHAPE, PLANES_SHAPE),
        scratch_shapes=[pltpu.VMEM((512, 512), F32), pltpu.VMEM((2, 128, 128), F32)],
        compiler_params=params(),
        name=name,
    )(planes, weight, table("zf"), table("zi"))


def weight_grad(spec, grad):
    return pl.pallas_call(
        weight_grad_kernel,
        out_shape=jax.ShapeDtypeStruct((2, C, C, M * M), F32),
        compiler_params=params(),
        name="weight_grad",
    )(spec, grad)


def outputs(planes, fields, cotangent, pw):
    return pl.pallas_call(
        output_kernel,
        grid=(4,),
        in_specs=[
            LANE_BLOCK,
            GRID_FULL,
            GRID_BLOCK,
            pl.BlockSpec((64, 256), lambda i: (i, 0)),
            whole((2, 1024, 256)),
            whole((128, 192)),
            whole((128, 256)),
            whole((2, 1024, 256)),
        ],
        out_specs=(
            GRID_BLOCK,
            GRID_BLOCK,
            GRID_BLOCK,
            LANE_BLOCK,
            pl.BlockSpec((1, 4, 256), lambda i: (i, 0, 0)),
        ),
        out_shape=(
            GRID_SHAPE,
            GRID_SHAPE,
            GRID_SHAPE,
            PLANES_SHAPE,
            jax.ShapeDtypeStruct((4, 4, 256), F32),
        ),
        scratch_shapes=[
            pltpu.VMEM((ZL, 4, X, Y), F32),
            pltpu.VMEM((256, 1024), BF),
            pltpu.VMEM((256, 1024), BF),
            pltpu.VMEM((128, 256), F32),
        ],
        compiler_params=params(),
        name="outputs",
    )(planes, fields, cotangent, pw, table("yi"), table("xi"), table("xg"), table("yf"))


def input_grads(planes, high, low, pw):
    return pl.pallas_call(
        input_kernel,
        grid=(4,),
        in_specs=[
            LANE_BLOCK,
            GRID_FULL,
            GRID_FULL,
            pl.BlockSpec((64, 256), lambda i: (i, 0)),
            whole((2, 1024, 256)),
            whole((128, 192)),
        ],
        out_specs=GRID_BLOCK,
        out_shape=GRID_SHAPE,
        scratch_shapes=[pltpu.VMEM((ZL, 4, X, Y), F32)],
        compiler_params=params(),
        name="input_grads",
    )(planes, high, low, pw, table("yi"), table("xj"))


def exchange(planes):
    return lax.all_to_all(planes, "gz", 0, 0, tiled=True)


def shards(fields, cotangent, spectral_weight, pointwise_weight):
    eye = jnp.eye(16, dtype=BF)
    to_out = jnp.kron(pointwise_weight.T, eye)
    to_in = jnp.kron(pointwise_weight, eye)
    planes = exchange(field_forward(fields))
    spec, back = mode_call(mix_kernel, "mix", planes, spectral_weight)
    act, high, low, grad_planes, point = outputs(exchange(back), fields, cotangent, to_out)
    grad_spec, back = mode_call(adjoint_kernel, "adjoint", exchange(grad_planes), spectral_weight)
    grad_input = input_grads(exchange(back), high, low, to_in)
    spectral_grad = weight_grad(lax.all_gather(spec, "dp"), lax.all_gather(grad_spec, "dp"))
    point = point.reshape(C, C, 16).sum(-1).T
    pointwise_grad = lax.psum(point, ("dp", "gz")) * (1.0 / math.sqrt(CELLS))
    return act, grad_input, pointwise_grad, spectral_grad


def solution(mesh):
    placed = (
        P("dp", "gz", None, None, None),
        P("dp", "gz", None, None, None),
        P(None, None, None, "gz"),
        P(),
    )
    return jax.shard_map(
        shards,
        mesh=mesh,
        in_specs=placed,
        out_specs=(
            P("dp", "gz", None, None, None),
            P("dp", "gz", None, None, None),
            P(),
            P(None, None, None, "gz"),
        ),
        check_vma=False,
    )
```

```python
import math

import jax
import jax.numpy as jnp
import ml_dtypes
import numpy as np
from jax import lax
from jax.experimental import pallas as pl
from jax.experimental.pallas import tpu as pltpu
from jax.sharding import PartitionSpec as P

M = 32
C = 16
ZL = 8
X = 128
Y = 128
Z = 256
GROUPS = 32
SAMPLES = 4
MODES = M * M * M
CELLS = SAMPLES * X * Y * Z
SCALE = 1.0 / math.sqrt(X * Y * Z * MODES)
BF = jnp.bfloat16
F32 = jnp.float32
VMEM_LIMIT = 62 * 1024 * 1024
K0 = math.sqrt(2.0 / math.pi)
K1 = K0 * 0.044715
MESH = pl.DeviceIdType.MESH


def halves(table):
    high = table.astype(ml_dtypes.bfloat16)
    low = (table - high.astype(np.float64)).astype(ml_dtypes.bfloat16)
    return high, low


def wave(length, left, right):
    phase = np.outer(left, right) % length
    angle = phase * (2.0 * np.pi / length)
    return np.cos(angle), np.sin(angle)


def make_tables():
    modes = np.arange(M)
    ky = 4 * (modes % 8) + modes // 8
    tables = {}
    cos_y, sin_y = wave(Y, ky, np.arange(Y))
    high, low = halves(np.concatenate([cos_y, -sin_y]))
    tables["yf"] = np.concatenate([high, low])
    tables["yg"] = np.concatenate(
        [np.concatenate([high, high], 1), np.concatenate([low, np.zeros_like(low)], 1)]
    )
    cos_x, sin_x = wave(X, modes, np.arange(X))
    high, low = halves(
        np.concatenate(
            [np.concatenate([cos_x, sin_x], 1), np.concatenate([-sin_x, cos_x], 1)]
        )
    )
    tables["xf"] = np.concatenate([high, low])
    high, low = halves(
        np.concatenate(
            [np.concatenate([cos_y, sin_y], 1), np.concatenate([-sin_y, cos_y], 1)]
        )
    )
    zero = np.zeros_like(low)
    tables["yi"] = np.stack(
        [np.concatenate([high, high, low, zero]), np.concatenate([high, high, zero, low])]
    )
    for name, scale in (("xi", SCALE), ("xj", 1.0)):
        high, low = halves(scale * np.concatenate([cos_x, -sin_x]).T)
        tables[name] = np.concatenate([high, high, low], 1)
    cos_z, sin_z = wave(Z, np.arange(Z), np.tile(modes, 4))
    tables["zf"] = np.stack(
        halves(
            np.concatenate(
                [np.concatenate([cos_z, -sin_z], 1), np.concatenate([sin_z, cos_z], 1)]
            )
        )
    )
    tables["zi"] = np.stack(halves(np.concatenate([cos_z, sin_z], 1)))
    return tables


TABLES = make_tables()
NAMES = ("yf", "yg", "xf", "yi", "xi", "xj", "zf", "zi")


def dot(a, b):
    return lax.dot_general(a, b, (((1,), (0,)), ((), ())), preferred_element_type=F32)


def dot_nt(a, b, precision=None):
    return lax.dot_general(
        a, b, (((1,), (1,)), ((), ())), preferred_element_type=F32, precision=precision
    )


def split(values):
    high = values.astype(BF)
    return high, (values - high.astype(F32)).astype(BF)


def side(arrays):
    return jnp.concatenate(arrays, axis=1)


def stack(arrays):
    return jnp.concatenate(arrays, axis=0)


def forward_x(sections, xf, out, group, zp):
    rows = []
    for zz in range(2):
        at = slice(zz * X, (zz + 1) * X)
        rows += [side([section[:M, at], section[M:, at]]) for section in sections]
    high, low = split(stack(rows))
    wide = dot_nt(xf[...], high)
    total = wide[:64] + wide[64:] + dot_nt(xf[0:64, :], low)
    flat = out.reshape(GROUPS * 64, 128)
    for zz in range(2):
        for part in range(2):
            first = group * 16 + part * ZL + 2 * zp + zz
            flat[pl.ds(first, M, stride=64), :] = total[
                part * M : (part + 1) * M, zz * 128 : (zz + 1) * 128
            ]


def field_forward(field, yf, xf, out, group):
    @pl.loop(0, ZL // 2)
    def _(zp):
        sections = []
        for k in range(4):
            c = group * 4 + k
            both = dot_nt(yf[...], stack([field[2 * zp, c], field[2 * zp + 1, c]]))
            sections.append(both[:64] + both[64:])
        forward_x(sections, xf, out, group, zp)


def depth_rows(planes, rows, group):
    for part in range(2):
        turned = planes[:, group, part * ZL : (part + 1) * ZL, :].reshape(Z, 128).T
        for k in range(4):
            for j in range(4):
                at = pl.multiple_of(j * 128 + (group * 4 + k) * 8, 8)
                rows[pl.ds(at, 8), part * 256 : (part + 1) * 256] = turned[
                    k * 32 + j * 8 : k * 32 + j * 8 + 8
                ]


def depth_forward(rows, zf):
    which = lax.broadcasted_iota(jnp.int32, (128, 256), 1) // 32 % 4
    total = None
    for j in range(4):
        high, low = split(rows[j * 128 : (j + 1) * 128, :])
        wide = dot(high, zf[0]) + dot(low, zf[0]) + dot(high, zf[1])
        total = wide if total is None else jnp.where(which == j, wide, total)
    return total


def depth_inverse(spectrum, zi, out, group):
    lane = lax.broadcasted_iota(jnp.int32, (8, 128), 1) // 32
    right = []
    for k in range(4):
        at = pl.ds(pl.multiple_of((group * 4 + k) * 8, 8), 8)
        real_in = spectrum[0, at, :]
        imag_in = spectrum[1, at, :]
        real_in = stack([jnp.where(lane == j, real_in, 0.0) for j in range(4)])
        imag_in = stack([jnp.where(lane == j, imag_in, 0.0) for j in range(4)])
        right += [side([real_in, -imag_in]), side([imag_in, real_in])]
    high, low = split(stack(right))
    total = dot_nt(zi[0], high) + dot_nt(zi[0], low) + dot_nt(zi[1], high)
    for pair in range(2):
        out[:, group, pair * ZL : (pair + 1) * ZL, :] = total[
            :, pair * 128 : (pair + 1) * 128
        ].reshape(GROUPS, ZL, 128)


def mix(spec, weight, mixed):
    @pl.loop(0, 8)
    def _(g):
        lanes = pl.ds(pl.multiple_of(g * 128, 128), 128)
        real_out = jnp.zeros((C, 128), F32)
        imag_out = jnp.zeros((C, 128), F32)
        for c in range(C):
            real_in = spec[0, pl.ds(c * 8 + g, 1), :]
            imag_in = spec[1, pl.ds(c * 8 + g, 1), :]
            wr = weight[0, c, :, lanes].astype(F32)
            wi = weight[1, c, :, lanes].astype(F32)
            real_out += real_in * wr - imag_in * wi
            imag_out += real_in * wi + imag_in * wr
        mixed[0, pl.ds(g, C, stride=8), :] = real_out
        mixed[1, pl.ds(g, C, stride=8), :] = imag_out


def mix_adjoint(spec, weight, mixed):
    @pl.loop(0, 8)
    def _(g):
        lanes = pl.ds(pl.multiple_of(g * 128, 128), 128)
        real_in = spec[0, pl.ds(g, C, stride=8), :]
        imag_in = spec[1, pl.ds(g, C, stride=8), :]
        for c in range(C):
            wr = weight[0, c, :, lanes].astype(F32)
            wi = weight[1, c, :, lanes].astype(F32)
            at = pl.ds(c * 8 + g, 1)
            mixed[0, at, :] = jnp.sum(real_in * wr + imag_in * wi, axis=0, keepdims=True)
            mixed[1, at, :] = jnp.sum(imag_in * wr - real_in * wi, axis=0, keepdims=True)


def weight_grad(spec, grad, out):
    factor = math.sqrt(MODES / CELLS)

    @pl.loop(0, 8)
    def _(g):
        lanes = pl.ds(pl.multiple_of(g * 128, 128), 128)
        grads = [
            [grad[s, part, pl.ds(g, C, stride=8), :] * factor for part in range(2)]
            for s in range(SAMPLES)
        ]
        for c in range(C):
            real_out = jnp.zeros((C, 128), F32)
            imag_out = jnp.zeros((C, 128), F32)
            for s in range(SAMPLES):
                ur = spec[s, 0, pl.ds(c * 8 + g, 1), :]
                ui = spec[s, 1, pl.ds(c * 8 + g, 1), :]
                gr, gi = grads[s]
                real_out += ur * gr + ui * gi
                imag_out += ur * gi - ui * gr
            out[0, c, :, lanes] = real_out
            out[1, c, :, lanes] = imag_out


def inverse_y(planes, yi, middle, group):
    flat = planes.reshape(GROUPS * 64, 128)
    lane = lax.broadcasted_iota(jnp.int32, (256, 128), 1)
    for pair in range(2):
        values = stack(
            [flat[pl.ds(group * 16 + pair * ZL + z, M, stride=64), :] for z in range(ZL)]
        )
        high = values.astype(BF)
        wide = high.astype(F32)
        turned = pltpu.roll(values - wide, 64, 1)
        even = jnp.where(lane < 64, wide, turned).astype(BF)
        odd = jnp.where(lane < 64, turned, wide).astype(BF)
        middle[2 * pair] = dot(side([even, high]), yi[0])
        middle[2 * pair + 1] = dot(side([odd, high]), yi[1])


def inverse_x(middle, table, zp, k):
    first = middle[k, pl.ds(pl.multiple_of(2 * zp * M, M), M), :]
    second = middle[k, pl.ds(pl.multiple_of((2 * zp + 1) * M, M), M), :]
    high, low = split(
        stack([side([first[:, :Y], second[:, :Y]]), side([first[:, Y:], second[:, Y:]])])
    )
    return dot(table[...], stack([high, low, high]))


def cells_of(ref, zp, rows):
    return side([ref[2 * zp + zz, :, rows, :].reshape(C * 16, Y) for zz in range(2)])


def spread(ref, lefts, local):
    @pl.loop(0, X // 16)
    def _(xb):
        rows = pl.ds(pl.multiple_of(xb * 16, 16), 16)
        for zp in range(ZL // 2):
            total = None
            for source in lefts:
                term = dot(ref[...], cells_of(source, zp, rows))
                total = term if total is None else total + term
            for zz in range(2):
                local[2 * zp + zz, :, rows, :] = total[:, zz * Y : (zz + 1) * Y].reshape(
                    C, 16, Y
                )


def step_kernel(*refs):
    fields, cotangent, weights, pointwise = refs[:4]
    sources = dict(zip(NAMES, refs[4 : 4 + len(NAMES)]))
    refs = refs[4 + len(NAMES) :]
    act_out, grad_out, point_out, spec_grad_out = refs[:4]
    refs = refs[4:]
    tables = dict(zip(NAMES, refs[: len(NAMES)]))
    refs = refs[len(NAMES) :]
    (
        field, cot, weight, act, grad_in, high_g, low_g, local,
        send_a, recv_a, send_b, recv_b, send_c, recv_c, send_d, recv_d,
        specs, grads, mixed, rows_ref, middle, spread_out, spread_in, point_acc, spec_grad,
        point_z, point_y, point_x,
        load_sem, store_sem, send_sem, recv_sem, small_send, small_recv,
    ) = refs
    me = lax.axis_index("gz")
    dp = lax.axis_index("dp")

    barrier = pltpu.get_barrier_semaphore()

    @pl.loop(1, GROUPS)
    def _(k):
        pl.semaphore_signal(
            barrier, inc=1, device_id=(dp, lax.rem(me + k, GROUPS)), device_id_type=MESH
        )

    for k in range(1, SAMPLES):
        pl.semaphore_signal(
            barrier, inc=1, device_id=(lax.rem(dp + k, SAMPLES), me), device_id_type=MESH
        )

    def channels(group):
        return pl.ds(group * 4, 4)

    def field_load(group):
        return pltpu.make_async_copy(
            fields.at[0, :, channels(group)], field.at[:, channels(group)], load_sem.at[group]
        )

    def cot_load(group):
        return pltpu.make_async_copy(
            cotangent.at[0, :, channels(group)], cot.at[:, channels(group)], load_sem.at[4 + group]
        )

    def table_load(name):
        return pltpu.make_async_copy(
            sources[name], tables[name], load_sem.at[8 + NAMES.index(name)]
        )

    weight_load = pltpu.make_async_copy(weights, weight, load_sem.at[16])
    for name in ("yf", "xf"):
        table_load(name).start()
    for group in range(4):
        field_load(group).start()
    for name in NAMES:
        if name not in ("yf", "xf"):
            table_load(name).start()
    weight_load.start()
    for group in range(4):
        cot_load(group).start()

    def send(index, group, source, target):
        @pl.loop(1, GROUPS)
        def _(k):
            peer = lax.rem(me + k, GROUPS)
            pltpu.make_async_remote_copy(
                src_ref=source.at[peer, group],
                dst_ref=target.at[me, group],
                send_sem=send_sem.at[index, group],
                recv_sem=recv_sem.at[index, group],
                device_id=(dp, peer),
                device_id_type=MESH,
            ).start()

        target[me, group] = source[me, group]

    def wait_planes(sem, index, group, buffer):
        part = buffer.at[pl.ds(0, GROUPS - 1), group]
        pltpu.make_async_copy(part, part, sem.at[index, group]).wait()

    def small(index, buffer, slot, count, place):
        for k in range(1, count):
            pltpu.make_async_remote_copy(
                src_ref=buffer.at[slot],
                dst_ref=buffer.at[slot],
                send_sem=small_send.at[index],
                recv_sem=small_recv.at[index],
                device_id=place(k),
                device_id_type=MESH,
            ).start()

    def small_wait(sem, index, buffer, count):
        part = buffer.at[pl.ds(0, count - 1)]
        pltpu.make_async_copy(part, part, sem.at[index]).wait()

    def along_dp(k):
        return lax.rem(dp + k, SAMPLES), me

    def along_z(k):
        return dp, me // 8 * 8 + lax.rem(me + k, 8)

    def along_y(k):
        return dp, lax.rem(me + 8 * k, GROUPS)

    for name in ("yf", "xf"):
        table_load(name).wait()

    field_load(0).wait()
    field_forward(field, tables["yf"], tables["xf"], send_a, 0)
    pl.semaphore_wait(barrier, GROUPS - 1 + SAMPLES - 1)
    send(0, 0, send_a, recv_a)

    @pl.loop(1, 4)
    def _(group):
        field_load(group).wait()
        field_forward(field, tables["yf"], tables["xf"], send_a, group)
        send(0, group, send_a, recv_a)

    place = lax.broadcasted_iota(jnp.int32, (256, C), 0) // 16
    one_hot = (place == lax.broadcasted_iota(jnp.int32, (256, C), 1)).astype(F32).astype(BF)
    same = (
        lax.broadcasted_iota(jnp.int32, (256, 256), 0) % 16
        == lax.broadcasted_iota(jnp.int32, (256, 256), 1) % 16
    )
    for left, target in (
        (dot_nt(one_hot, pointwise[...]), spread_out),
        (dot(one_hot, pointwise[...]), spread_in),
    ):
        target[...] = jnp.where(same, dot_nt(left.astype(BF), one_hot), 0.0).astype(BF)
    spread(spread_out, (field,), local)
    for name in NAMES:
        if name not in ("yf", "xf"):
            table_load(name).wait()
    weight_load.wait()

    @pl.loop(0, 4)
    def _(group):
        wait_planes(recv_sem, 0, group, recv_a)
        depth_rows(recv_a, rows_ref, group)

    spec = depth_forward(rows_ref, tables["zf"])
    specs[dp, 0] = spec[:, :128]
    specs[dp, 1] = spec[:, 128:]
    mix(specs.at[dp], weight, mixed)

    @pl.loop(0, 4)
    def _(group):
        depth_inverse(mixed, tables["zi"], send_b, group)
        send(1, group, send_b, recv_b)

    small(0, specs, dp, SAMPLES, along_dp)

    @pl.loop(0, 4)
    def _(group):
        wait_planes(recv_sem, 1, group, recv_b)
        inverse_y(recv_b, tables["yi"], middle, group)
        cot_load(group).wait()

        @pl.loop(0, ZL // 2)
        def _(zp):
            sections = []
            for k in range(4):
                o = group * 4 + k
                both = inverse_x(middle, tables["xi"], zp, k)
                right = []
                for zz in range(2):
                    z = 2 * zp + zz
                    values = both[:, zz * Y : (zz + 1) * Y] + local[z, o]
                    square = values * values
                    half = 0.5 + 0.5 * jnp.tanh(values * (K0 + K1 * square))
                    act[z, o] = (values * half).astype(BF)
                    slope = half + values * (2.0 * K0 + 6.0 * K1 * square) * (half - half * half)
                    high, low = split(cot[z, o].astype(F32) * slope)
                    high_g[z, o] = high
                    low_g[z, o] = low
                    right.append(side([high, low]))
                wide = dot_nt(tables["yg"][...], stack(right))
                sections.append(wide[:64] + wide[64:])
            forward_x(sections, tables["xf"], send_c, group, zp)

        send(2, group, send_c, recv_c)
        pltpu.make_async_copy(
            act.at[:, channels(group)], act_out.at[0, :, channels(group)], store_sem.at[0]
        ).start()

    point_acc[...] = jnp.zeros_like(point_acc)

    @pl.loop(0, X // 16)
    def _(xb):
        rows = pl.ds(pl.multiple_of(xb * 16, 16), 16)
        total = None
        for zp in range(ZL // 2):
            cells = cells_of(field, zp, rows)
            term = dot_nt(cells_of(high_g, zp, rows), cells)
            term += dot_nt(cells_of(low_g, zp, rows), cells)
            total = term if total is None else total + term
        point_acc[...] += total

    kept = jnp.where(same, point_acc[...], 0.0).reshape(C, 16, 256).sum(axis=1)
    groups = lax.broadcasted_iota(jnp.int32, (C, 256), 1) // 16
    picks = (groups == lax.broadcasted_iota(jnp.int32, (C, 256), 0)).astype(F32)
    kept = stack([kept, jnp.zeros((128 - C, 256), F32)])
    z_slot = lax.rem(me, 8)
    y_slot = me // 8
    point_z[z_slot] = dot_nt(picks, kept, lax.Precision.HIGHEST)
    small(1, point_z, z_slot, 8, along_z)

    @pl.loop(0, 4)
    def _(group):
        wait_planes(recv_sem, 2, group, recv_c)
        depth_rows(recv_c, rows_ref, group)

    spec = depth_forward(rows_ref, tables["zf"]) * SCALE
    grads[dp, 0] = spec[:, :128]
    grads[dp, 1] = spec[:, 128:]
    small(2, grads, dp, SAMPLES, along_dp)
    mix_adjoint(grads.at[dp], weight, mixed)

    @pl.loop(0, 4)
    def _(group):
        depth_inverse(mixed, tables["zi"], send_d, group)
        send(3, group, send_d, recv_d)

    small_wait(small_recv, 1, point_z, 8)
    point_y[y_slot] = jnp.sum(point_z[...], axis=0)
    small(3, point_y, y_slot, 4, along_y)
    spread(spread_in, (high_g, low_g), local)
    small_wait(small_recv, 3, point_y, 4)
    point_x[dp] = jnp.sum(point_y[...], axis=0)
    small(4, point_x, dp, SAMPLES, along_dp)
    small_wait(small_recv, 0, specs, SAMPLES)
    small_wait(small_recv, 2, grads, SAMPLES)
    weight_grad(specs, grads, spec_grad)
    spec_store = pltpu.make_async_copy(spec_grad, spec_grad_out, store_sem.at[2])
    spec_store.start()

    @pl.loop(0, 4)
    def _(group):
        wait_planes(recv_sem, 3, group, recv_d)
        inverse_y(recv_d, tables["yi"], middle, group)

        @pl.loop(0, ZL // 2)
        def _(zp):
            for k in range(4):
                c = group * 4 + k
                both = inverse_x(middle, tables["xj"], zp, k)
                for zz in range(2):
                    z = 2 * zp + zz
                    grad_in[z, c] = (both[:, zz * Y : (zz + 1) * Y] + local[z, c]).astype(BF)

        pltpu.make_async_copy(
            grad_in.at[:, channels(group)], grad_out.at[0, :, channels(group)], store_sem.at[1]
        ).start()

    small_wait(small_recv, 4, point_x, SAMPLES)
    total = jnp.sum(point_x[...], axis=0)
    point_out[...] = total[:, 0:C] * (1.0 / math.sqrt(CELLS))

    for index, buffer in enumerate((send_a, send_b, send_c, send_d)):
        @pl.loop(0, 4)
        def _(group):
            wait_planes(send_sem, index, group, buffer)

    for index, (buffer, count) in enumerate(
        ((specs, 4), (point_z, 8), (grads, 4), (point_y, 4), (point_x, 4))
    ):
        small_wait(small_send, index, buffer, count)
    spec_store.wait()
    pltpu.make_async_copy(act, act_out.at[0], store_sem.at[0]).wait()
    pltpu.make_async_copy(grad_in, grad_out.at[0], store_sem.at[1]).wait()


def shards(fields, cotangent, spectral_weight, pointwise_weight):
    tables = [jnp.asarray(TABLES[name]) for name in NAMES]
    grid_shape = (ZL, C, X, Y)
    planes = pltpu.VMEM((GROUPS, 4, 16, 128), F32)
    scratch = [pltpu.VMEM(table.shape, BF) for table in tables]
    scratch += [pltpu.VMEM(grid_shape, BF)] * 2
    scratch += [pltpu.VMEM((2, C, C, M * M), BF)]
    scratch += [pltpu.VMEM(grid_shape, BF)] * 4
    scratch += [pltpu.VMEM(grid_shape, F32)]
    scratch += [planes] * 8
    scratch += [pltpu.VMEM((SAMPLES, 2, 128, 128), F32)] * 2
    scratch += [
        pltpu.VMEM((2, 128, 128), F32),
        pltpu.VMEM((512, 512), F32),
        pltpu.VMEM((4, 256, 256), F32),
        pltpu.VMEM((256, 256), BF),
        pltpu.VMEM((256, 256), BF),
        pltpu.VMEM((256, 256), F32),
        pltpu.VMEM((2, C, C, M * M), F32),
        pltpu.VMEM((8, C, 128), F32),
        pltpu.VMEM((4, C, 128), F32),
        pltpu.VMEM((SAMPLES, C, 128), F32),
        pltpu.SemaphoreType.DMA((17,)),
        pltpu.SemaphoreType.DMA((3,)),
        pltpu.SemaphoreType.DMA((4, 4)),
        pltpu.SemaphoreType.DMA((4, 4)),
        pltpu.SemaphoreType.DMA((5,)),
        pltpu.SemaphoreType.DMA((5,)),
    ]
    anywhere = pl.BlockSpec(memory_space=pl.ANY)
    on_chip = pl.BlockSpec(memory_space=pltpu.VMEM)
    return pl.pallas_call(
        step_kernel,
        in_specs=[anywhere] * 3 + [on_chip] + [anywhere] * len(tables),
        out_specs=(anywhere, anywhere, on_chip, anywhere),
        out_shape=(
            jax.ShapeDtypeStruct((1,) + grid_shape, BF),
            jax.ShapeDtypeStruct((1,) + grid_shape, BF),
            jax.ShapeDtypeStruct((C, C), F32),
            jax.ShapeDtypeStruct((2, C, C, M * M), F32),
        ),
        scratch_shapes=scratch,
        compiler_params=pltpu.CompilerParams(
            vmem_limit_bytes=VMEM_LIMIT, collective_id=0, has_side_effects=True
        ),
        name="step",
    )(fields, cotangent, spectral_weight, pointwise_weight, *tables)


def solution(mesh):
    placed = (
        P("dp", "gz", None, None, None),
        P("dp", "gz", None, None, None),
        P(None, None, None, "gz"),
        P(),
    )
    return jax.shard_map(
        shards,
        mesh=mesh,
        in_specs=placed,
        out_specs=(
            P("dp", "gz", None, None, None),
            P("dp", "gz", None, None, None),
            P(),
            P(None, None, None, "gz"),
        ),
        check_vma=False,
    )
```

```python
import math

import jax
import jax.numpy as jnp
import ml_dtypes
import numpy as np
from jax import lax
from jax.experimental import pallas as pl
from jax.experimental.pallas import tpu as pltpu
from jax.sharding import PartitionSpec as P

M = 32
C = 16
ZL = 8
X = 128
Y = 128
Z = 256
GROUPS = 32
SAMPLES = 4
MODES = M * M * M
CELLS = SAMPLES * X * Y * Z
SCALE = 1.0 / math.sqrt(X * Y * Z * MODES)
BF = jnp.bfloat16
F32 = jnp.float32
VMEM_LIMIT = 48 * 1024 * 1024
K0 = math.sqrt(2.0 / math.pi)
K1 = K0 * 0.044715
GRAD = 1.5
MESH = pl.DeviceIdType.MESH


def halves(table):
    high = table.astype(ml_dtypes.bfloat16)
    low = (table - high.astype(np.float64)).astype(ml_dtypes.bfloat16)
    return high, low


def wave(length, left, right):
    phase = np.outer(left, right) % length
    angle = phase * (2.0 * np.pi / length)
    return np.cos(angle), np.sin(angle)


def make_tables():
    modes = np.arange(M)
    ky = 4 * (modes % 8) + modes // 8
    tables = {}
    cos_y, sin_y = wave(Y, ky, np.arange(Y))
    high, low = halves(np.concatenate([cos_y, -sin_y]))
    tables["yf"] = np.concatenate([high, low])
    high, low = halves(GRAD * np.concatenate([cos_y, -sin_y]))
    tables["yg"] = np.concatenate(
        [np.concatenate([high, high], 1), np.concatenate([low, np.zeros_like(low)], 1)]
    )
    cos_x, sin_x = wave(X, modes, np.arange(X))
    high, low = halves(
        np.concatenate(
            [np.concatenate([cos_x, sin_x], 1), np.concatenate([-sin_x, cos_x], 1)]
        )
    )
    tables["xf"] = np.concatenate([high, low])
    high, low = halves(
        np.concatenate(
            [np.concatenate([cos_y, sin_y], 1), np.concatenate([-sin_y, cos_y], 1)]
        )
    )
    zero = np.zeros_like(low)
    tables["yi"] = np.stack(
        [np.concatenate([high, high, low, zero]), np.concatenate([high, high, zero, low])]
    )
    for name, scale in (("xi", 0.5 * SCALE), ("xj", 1.0)):
        high, low = halves(scale * np.concatenate([cos_x, -sin_x]).T)
        tables[name] = np.concatenate([high, high, low], 1)
    cos_z, sin_z = wave(Z, np.arange(Z), np.tile(modes, 4))
    tables["zf"] = np.stack(
        halves(
            np.concatenate(
                [np.concatenate([cos_z, -sin_z], 1), np.concatenate([sin_z, cos_z], 1)]
            )
        )
    )
    tables["zi"] = np.stack(halves(np.concatenate([cos_z, sin_z], 1)))
    return tables


TABLES = make_tables()
NAMES = ("yf", "yg", "xf", "yi", "xi", "xj", "zf", "zi")


def dot(a, b):
    return lax.dot_general(a, b, (((1,), (0,)), ((), ())), preferred_element_type=F32)


def dot_nt(a, b, precision=None):
    return lax.dot_general(
        a, b, (((1,), (1,)), ((), ())), preferred_element_type=F32, precision=precision
    )


def split(values):
    high = values.astype(BF)
    return high, (values - high.astype(F32)).astype(BF)


def side(arrays):
    return jnp.concatenate(arrays, axis=1)


def stack(arrays):
    return jnp.concatenate(arrays, axis=0)


def forward_x(sections, xf, out, group, zp):
    rows = []
    for zz in range(2):
        at = slice(zz * X, (zz + 1) * X)
        rows += [side([section[:M, at], section[M:, at]]) for section in sections]
    high, low = split(stack(rows))
    wide = dot_nt(xf[...], high)
    total = wide[:64] + wide[64:] + dot_nt(xf[0:64, :], low)
    flat = out.reshape(GROUPS * 64, 128)
    for zz in range(2):
        for part in range(2):
            first = group * 16 + part * ZL + 2 * zp + zz
            flat[pl.ds(first, M, stride=64), :] = total[
                part * M : (part + 1) * M, zz * 128 : (zz + 1) * 128
            ]


def field_forward(field, yf, xf, out, group):
    @pl.loop(0, ZL // 2)
    def _(zp):
        sections = []
        for k in range(4):
            c = group * 4 + k
            both = dot_nt(yf[...], stack([field[2 * zp, c], field[2 * zp + 1, c]]))
            sections.append(both[:64] + both[64:])
        forward_x(sections, xf, out, group, zp)


def depth_rows(planes, rows, group):
    for part in range(2):
        turned = planes[:, group, part * ZL : (part + 1) * ZL, :].reshape(Z, 128).T
        for k in range(4):
            for j in range(4):
                at = pl.multiple_of(j * 128 + (group * 4 + k) * 8, 8)
                rows[pl.ds(at, 8), part * 256 : (part + 1) * 256] = turned[
                    k * 32 + j * 8 : k * 32 + j * 8 + 8
                ]


def depth_forward(rows, zf):
    which = lax.broadcasted_iota(jnp.int32, (128, 256), 1) // 32 % 4
    total = None
    for j in range(4):
        high, low = split(rows[j * 128 : (j + 1) * 128, :])
        wide = dot(high, zf[0]) + dot(low, zf[0]) + dot(high, zf[1])
        total = wide if total is None else jnp.where(which == j, wide, total)
    return total


def depth_inverse(spectrum, zi, out, group):
    lane = lax.broadcasted_iota(jnp.int32, (8, 128), 1) // 32
    right = []
    for k in range(4):
        at = pl.ds(pl.multiple_of((group * 4 + k) * 8, 8), 8)
        real_in = spectrum[0, at, :]
        imag_in = spectrum[1, at, :]
        real_in = stack([jnp.where(lane == j, real_in, 0.0) for j in range(4)])
        imag_in = stack([jnp.where(lane == j, imag_in, 0.0) for j in range(4)])
        right += [side([real_in, -imag_in]), side([imag_in, real_in])]
    high, low = split(stack(right))
    total = dot_nt(zi[0], high) + dot_nt(zi[0], low) + dot_nt(zi[1], high)
    for pair in range(2):
        out[:, group, pair * ZL : (pair + 1) * ZL, :] = total[
            :, pair * 128 : (pair + 1) * 128
        ].reshape(GROUPS, ZL, 128)


def mix(spec, weight, mixed):
    @pl.loop(0, 8)
    def _(g):
        lanes = pl.ds(pl.multiple_of(g * 128, 128), 128)
        real_out = jnp.zeros((C, 128), F32)
        imag_out = jnp.zeros((C, 128), F32)
        for c in range(C):
            real_in = spec[0, pl.ds(c * 8 + g, 1), :]
            imag_in = spec[1, pl.ds(c * 8 + g, 1), :]
            wr = weight[0, c, :, lanes].astype(F32)
            wi = weight[1, c, :, lanes].astype(F32)
            real_out += real_in * wr - imag_in * wi
            imag_out += real_in * wi + imag_in * wr
        mixed[0, pl.ds(g, C, stride=8), :] = real_out
        mixed[1, pl.ds(g, C, stride=8), :] = imag_out


def mix_adjoint(spec, weight, mixed):
    @pl.loop(0, 8)
    def _(g):
        lanes = pl.ds(pl.multiple_of(g * 128, 128), 128)
        real_in = spec[0, pl.ds(g, C, stride=8), :]
        imag_in = spec[1, pl.ds(g, C, stride=8), :]
        for c in range(C):
            wr = weight[0, c, :, lanes].astype(F32)
            wi = weight[1, c, :, lanes].astype(F32)
            at = pl.ds(c * 8 + g, 1)
            mixed[0, at, :] = jnp.sum(real_in * wr + imag_in * wi, axis=0, keepdims=True)
            mixed[1, at, :] = jnp.sum(imag_in * wr - real_in * wi, axis=0, keepdims=True)


def weight_grad(spec, grad, out):
    factor = math.sqrt(MODES / CELLS)

    @pl.loop(0, 8)
    def _(g):
        lanes = pl.ds(pl.multiple_of(g * 128, 128), 128)
        grads = [
            [grad[s, part, pl.ds(g, C, stride=8), :] * factor for part in range(2)]
            for s in range(SAMPLES)
        ]
        for c in range(C):
            real_out = jnp.zeros((C, 128), F32)
            imag_out = jnp.zeros((C, 128), F32)
            for s in range(SAMPLES):
                ur = spec[s, 0, pl.ds(c * 8 + g, 1), :]
                ui = spec[s, 1, pl.ds(c * 8 + g, 1), :]
                gr, gi = grads[s]
                real_out += ur * gr + ui * gi
                imag_out += ur * gi - ui * gr
            out[0, c, :, lanes] = real_out
            out[1, c, :, lanes] = imag_out


def inverse_y(planes, yi, middle, group):
    flat = planes.reshape(GROUPS * 64, 128)
    lane = lax.broadcasted_iota(jnp.int32, (256, 128), 1)
    for pair in range(2):
        values = stack(
            [flat[pl.ds(group * 16 + pair * ZL + z, M, stride=64), :] for z in range(ZL)]
        )
        high = values.astype(BF)
        wide = high.astype(F32)
        turned = pltpu.roll(values - wide, 64, 1)
        even = jnp.where(lane < 64, wide, turned).astype(BF)
        odd = jnp.where(lane < 64, turned, wide).astype(BF)
        middle[2 * pair] = dot(side([even, high]), yi[0])
        middle[2 * pair + 1] = dot(side([odd, high]), yi[1])


def inverse_x(middle, table, zp, k):
    first = middle[k, pl.ds(pl.multiple_of(2 * zp * M, M), M), :]
    second = middle[k, pl.ds(pl.multiple_of((2 * zp + 1) * M, M), M), :]
    high, low = split(
        stack([side([first[:, :Y], second[:, :Y]]), side([first[:, Y:], second[:, Y:]])])
    )
    return dot(table[...], stack([high, low, high]))


def cells_of(ref, zp, rows):
    return side([ref[2 * zp + zz, :, rows, :].reshape(C * 16, Y) for zz in range(2)])


def spread(ref, lefts, local, scale):
    @pl.loop(0, X // 16)
    def _(xb):
        rows = pl.ds(pl.multiple_of(xb * 16, 16), 16)
        for zp in range(ZL // 2):
            total = None
            for source in lefts:
                term = dot(ref[...], cells_of(source, zp, rows))
                total = term if total is None else total + term
            for zz in range(2):
                local[2 * zp + zz, :, rows, :] = (
                    total[:, zz * Y : (zz + 1) * Y] * scale
                ).reshape(C, 16, Y)


def step_kernel(*refs):
    fields, cotangent, weights, pointwise = refs[:4]
    sources = dict(zip(NAMES, refs[4 : 4 + len(NAMES)]))
    refs = refs[4 + len(NAMES) :]
    act_out, grad_out, point_out, spec_grad = refs[:4]
    act, grad_in = act_out.at[0], grad_out.at[0]
    refs = refs[4:]
    tables = dict(zip(NAMES, refs[: len(NAMES)]))
    refs = refs[len(NAMES) :]
    (
        field, cot, weight, high_g, low_g, local,
        send_a, recv_a, send_b, recv_b, send_c, recv_c, send_d, recv_d,
        specs, grads, mixed, rows_ref, middle, spread_out, spread_in, point_acc,
        point_z, point_y, point_x, pre,
        load_sem, send_sem, recv_sem, small_send, small_recv,
    ) = refs
    me = lax.axis_index("gz")
    dp = lax.axis_index("dp")

    barrier = pltpu.get_barrier_semaphore()

    @pl.loop(1, GROUPS)
    def _(k):
        pl.semaphore_signal(
            barrier, inc=1, device_id=(dp, lax.rem(me + k, GROUPS)), device_id_type=MESH
        )

    for k in range(1, SAMPLES):
        pl.semaphore_signal(
            barrier, inc=1, device_id=(lax.rem(dp + k, SAMPLES), me), device_id_type=MESH
        )

    def channels(group):
        return pl.ds(group * 4, 4)

    def field_load(group):
        return pltpu.make_async_copy(
            fields.at[0, :, channels(group)], field.at[:, channels(group)], load_sem.at[group]
        )

    def cot_load(group):
        return pltpu.make_async_copy(
            cotangent.at[0, :, channels(group)], cot.at[:, channels(group)], load_sem.at[4 + group]
        )

    def table_load(name):
        return pltpu.make_async_copy(
            sources[name], tables[name], load_sem.at[8 + NAMES.index(name)]
        )

    weight_load = pltpu.make_async_copy(weights, weight, load_sem.at[16])
    for name in ("yf", "xf"):
        table_load(name).start()
    for group in range(4):
        field_load(group).start()
    for name in NAMES:
        if name not in ("yf", "xf"):
            table_load(name).start()
    weight_load.start()
    for group in range(4):
        cot_load(group).start()

    def send(index, group, source, target):
        @pl.loop(1, GROUPS)
        def _(k):
            peer = lax.rem(me + k, GROUPS)
            pltpu.make_async_remote_copy(
                src_ref=source.at[peer, group],
                dst_ref=target.at[me, group],
                send_sem=send_sem.at[index, group],
                recv_sem=recv_sem.at[index, group],
                device_id=(dp, peer),
                device_id_type=MESH,
            ).start()

        target[me, group] = source[me, group]

    def wait_planes(sem, index, group, buffer):
        part = buffer.at[pl.ds(0, GROUPS - 1), group]
        pltpu.make_async_copy(part, part, sem.at[index, group]).wait()

    def small(index, buffer, slot, count, place):
        for k in range(1, count):
            pltpu.make_async_remote_copy(
                src_ref=buffer.at[slot],
                dst_ref=buffer.at[slot],
                send_sem=small_send.at[index],
                recv_sem=small_recv.at[index],
                device_id=place(k),
                device_id_type=MESH,
            ).start()

    def small_wait(sem, index, buffer, count):
        part = buffer.at[pl.ds(0, count - 1)]
        pltpu.make_async_copy(part, part, sem.at[index]).wait()

    def along_dp(k):
        return lax.rem(dp + k, SAMPLES), me

    def along_z(k):
        return dp, me // 8 * 8 + lax.rem(me + k, 8)

    def along_y(k):
        return dp, lax.rem(me + 8 * k, GROUPS)

    for name in ("yf", "xf"):
        table_load(name).wait()

    field_load(0).wait()
    field_forward(field, tables["yf"], tables["xf"], send_a, 0)
    pl.semaphore_wait(barrier, GROUPS - 1 + SAMPLES - 1)
    send(0, 0, send_a, recv_a)

    @pl.loop(1, 4)
    def _(group):
        field_load(group).wait()
        field_forward(field, tables["yf"], tables["xf"], send_a, group)
        send(0, group, send_a, recv_a)

    place = lax.broadcasted_iota(jnp.int32, (256, C), 0) // 16
    one_hot = (place == lax.broadcasted_iota(jnp.int32, (256, C), 1)).astype(F32).astype(BF)
    same = (
        lax.broadcasted_iota(jnp.int32, (256, 256), 0) % 16
        == lax.broadcasted_iota(jnp.int32, (256, 256), 1) % 16
    )
    for left, target in (
        (dot_nt(one_hot, pointwise[...]), spread_out),
        (dot(one_hot, pointwise[...]), spread_in),
    ):
        target[...] = jnp.where(same, dot_nt(left.astype(BF), one_hot), 0.0).astype(BF)
    spread(spread_out, (field,), local, 0.5)
    for name in NAMES:
        if name not in ("yf", "xf"):
            table_load(name).wait()
    weight_load.wait()

    @pl.loop(0, 4)
    def _(group):
        wait_planes(recv_sem, 0, group, recv_a)
        depth_rows(recv_a, rows_ref, group)

    spec = depth_forward(rows_ref, tables["zf"])
    specs[dp, 0] = spec[:, :128]
    specs[dp, 1] = spec[:, 128:]
    mix(specs.at[dp], weight, mixed)

    @pl.loop(0, 4)
    def _(group):
        depth_inverse(mixed, tables["zi"], send_b, group)
        send(1, group, send_b, recv_b)

    small(0, specs, dp, SAMPLES, along_dp)

    @pl.loop(0, 4)
    def _(group):
        wait_planes(recv_sem, 1, group, recv_b)
        inverse_y(recv_b, tables["yi"], middle, group)
        cot_load(group).wait()

        for zp in range(ZL // 2 + 2):
            sections = []
            for k in range(4):
                o = group * 4 + k
                if zp < ZL // 2:
                    both = inverse_x(middle, tables["xi"], zp, k)
                    for zz in range(2):
                        pre[zp % 2, k, zz] = both[:, zz * Y : (zz + 1) * Y]
                if 1 <= zp <= ZL // 2:
                    for zz in range(2):
                        z = 2 * (zp - 1) + zz
                        values = pre[(zp - 1) % 2, k, zz] + local[z, o]
                        inner = values * (2.0 * K0 + 8.0 * K1 * (values * values))
                        wave_t = jnp.tanh(inner)
                        twice = 1.0 + wave_t
                        act[z, o] = (values * twice).astype(BF)
                        slope = 1.0 / 3.0 + (inner - (4.0 / 3.0 * K0) * values) * (1.0 - wave_t)
                        high, low = split(cot[z, o].astype(F32) * twice * slope)
                        high_g[z, o] = high
                        low_g[z, o] = low
                if 2 <= zp:
                    right = [
                        side([high_g[2 * (zp - 2) + zz, o], low_g[2 * (zp - 2) + zz, o]])
                        for zz in range(2)
                    ]
                    wide = dot_nt(tables["yg"][...], stack(right))
                    sections.append(wide[:64] + wide[64:])
            if 2 <= zp:
                forward_x(sections, tables["xf"], send_c, group, zp - 2)

        send(2, group, send_c, recv_c)

    point_acc[...] = jnp.zeros_like(point_acc)

    @pl.loop(0, X // 16)
    def _(xb):
        rows = pl.ds(pl.multiple_of(xb * 16, 16), 16)
        total = None
        for zp in range(ZL // 2):
            cells = cells_of(field, zp, rows)
            term = dot_nt(cells_of(high_g, zp, rows), cells)
            term += dot_nt(cells_of(low_g, zp, rows), cells)
            total = term if total is None else total + term
        point_acc[...] += total

    kept = jnp.where(same, point_acc[...], 0.0).reshape(C, 16, 256).sum(axis=1)
    groups = lax.broadcasted_iota(jnp.int32, (C, 256), 1) // 16
    picks = (groups == lax.broadcasted_iota(jnp.int32, (C, 256), 0)).astype(F32)
    kept = stack([kept, jnp.zeros((128 - C, 256), F32)])
    z_slot = lax.rem(me, 8)
    y_slot = me // 8
    point_z[z_slot] = dot_nt(picks, kept, lax.Precision.HIGHEST)
    small(1, point_z, z_slot, 8, along_z)

    @pl.loop(0, 4)
    def _(group):
        wait_planes(recv_sem, 2, group, recv_c)
        depth_rows(recv_c, rows_ref, group)

    spec = depth_forward(rows_ref, tables["zf"]) * SCALE
    grads[dp, 0] = spec[:, :128]
    grads[dp, 1] = spec[:, 128:]
    small(2, grads, dp, SAMPLES, along_dp)
    mix_adjoint(grads.at[dp], weight, mixed)

    @pl.loop(0, 4)
    def _(group):
        depth_inverse(mixed, tables["zi"], send_d, group)
        send(3, group, send_d, recv_d)

    small_wait(small_recv, 1, point_z, 8)
    point_y[y_slot] = jnp.sum(point_z[...], axis=0)
    small(3, point_y, y_slot, 4, along_y)
    spread(spread_in, (high_g, low_g), local, GRAD)
    small_wait(small_recv, 3, point_y, 4)
    point_x[dp] = jnp.sum(point_y[...], axis=0)
    small(4, point_x, dp, SAMPLES, along_dp)
    small_wait(small_recv, 0, specs, SAMPLES)
    small_wait(small_recv, 2, grads, SAMPLES)
    weight_grad(specs, grads, spec_grad)

    @pl.loop(0, 4)
    def _(group):
        wait_planes(recv_sem, 3, group, recv_d)
        inverse_y(recv_d, tables["yi"], middle, group)

        @pl.loop(0, ZL // 2)
        def _(zp):
            for k in range(4):
                c = group * 4 + k
                both = inverse_x(middle, tables["xj"], zp, k)
                for zz in range(2):
                    z = 2 * zp + zz
                    grad_in[z, c] = (both[:, zz * Y : (zz + 1) * Y] + local[z, c]).astype(BF)

    small_wait(small_recv, 4, point_x, SAMPLES)
    total = jnp.sum(point_x[...], axis=0)
    point_out[...] = total[:, 0:C] * (GRAD / math.sqrt(CELLS))

    for index, buffer in enumerate((send_a, send_b, send_c, send_d)):
        @pl.loop(0, 4)
        def _(group):
            wait_planes(send_sem, index, group, buffer)

    for index, (buffer, count) in enumerate(
        ((specs, 4), (point_z, 8), (grads, 4), (point_y, 4), (point_x, 4))
    ):
        small_wait(small_send, index, buffer, count)


def store_kernel(*refs):
    copies = [
        pltpu.make_async_copy(refs[i], refs[4 + i], refs[8].at[i]) for i in range(4)
    ]
    for copy in copies:
        copy.start()
    for copy in copies:
        copy.wait()


def shards(fields, cotangent, spectral_weight, pointwise_weight):
    tables = [jnp.asarray(TABLES[name]) for name in NAMES]
    grid_shape = (ZL, C, X, Y)
    planes = pltpu.VMEM((GROUPS, 4, 16, 128), F32)
    scratch = [pltpu.VMEM(table.shape, BF) for table in tables]
    scratch += [pltpu.VMEM(grid_shape, BF)] * 2
    scratch += [pltpu.VMEM((2, C, C, M * M), BF)]
    scratch += [pltpu.VMEM(grid_shape, BF)] * 2
    scratch += [pltpu.VMEM(grid_shape, F32)]
    scratch += [planes] * 8
    scratch += [pltpu.VMEM((SAMPLES, 2, 128, 128), F32)] * 2
    scratch += [
        pltpu.VMEM((2, 128, 128), F32),
        pltpu.VMEM((512, 512), F32),
        pltpu.VMEM((4, 256, 256), F32),
        pltpu.VMEM((256, 256), BF),
        pltpu.VMEM((256, 256), BF),
        pltpu.VMEM((256, 256), F32),
        pltpu.VMEM((8, C, 128), F32),
        pltpu.VMEM((4, C, 128), F32),
        pltpu.VMEM((SAMPLES, C, 128), F32),
        pltpu.VMEM((2, 4, 2, X, Y), F32),
        pltpu.SemaphoreType.DMA((17,)),
        pltpu.SemaphoreType.DMA((4, 4)),
        pltpu.SemaphoreType.DMA((4, 4)),
        pltpu.SemaphoreType.DMA((5,)),
        pltpu.SemaphoreType.DMA((5,)),
    ]
    anywhere = pl.BlockSpec(memory_space=pl.ANY)
    on_chip = pl.BlockSpec(memory_space=pltpu.VMEM)
    shapes = (
        jax.ShapeDtypeStruct((1,) + grid_shape, BF),
        jax.ShapeDtypeStruct((1,) + grid_shape, BF),
        jax.ShapeDtypeStruct((C, C), F32),
        jax.ShapeDtypeStruct((2, C, C, M * M), F32),
    )
    results = pl.pallas_call(
        step_kernel,
        in_specs=[anywhere] * 3 + [on_chip] + [anywhere] * len(tables),
        out_specs=(on_chip,) * 4,
        out_shape=tuple(pltpu.VMEM(shape.shape, shape.dtype) for shape in shapes),
        scratch_shapes=scratch,
        compiler_params=pltpu.CompilerParams(
            vmem_limit_bytes=VMEM_LIMIT, collective_id=0, has_side_effects=True
        ),
        name="step",
    )(fields, cotangent, spectral_weight, pointwise_weight, *tables)
    return pl.pallas_call(
        store_kernel,
        in_specs=[on_chip] * 4,
        out_specs=(anywhere,) * 4,
        out_shape=shapes,
        scratch_shapes=[pltpu.SemaphoreType.DMA((4,))],
        compiler_params=pltpu.CompilerParams(vmem_limit_bytes=1024 * 1024),
        name="store",
    )(*results)


def solution(mesh):
    placed = (
        P("dp", "gz", None, None, None),
        P("dp", "gz", None, None, None),
        P(None, None, None, "gz"),
        P(),
    )
    return jax.shard_map(
        shards,
        mesh=mesh,
        in_specs=placed,
        out_specs=(
            P("dp", "gz", None, None, None),
            P("dp", "gz", None, None, None),
            P(),
            P(None, None, None, "gz"),
        ),
        check_vma=False,
    )
```

```python
import math

import jax
import jax.numpy as jnp
import ml_dtypes
import numpy as np
from jax import lax
from jax.experimental import pallas as pl
from jax.experimental.pallas import tpu as pltpu
from jax.sharding import PartitionSpec as P

M = 32
C = 16
ZL = 8
X = 128
Y = 128
Z = 256
GROUPS = 32
SAMPLES = 4
MODES = M * M * M
CELLS = SAMPLES * X * Y * Z
SCALE = 1.0 / math.sqrt(X * Y * Z * MODES)
BF = jnp.bfloat16
F32 = jnp.float32
VMEM_LIMIT = 42 * 1024 * 1024
K0 = math.sqrt(2.0 / math.pi)
K1 = K0 * 0.044715
GRAD = 1.5
MESH = pl.DeviceIdType.MESH


def halves(table):
    high = table.astype(ml_dtypes.bfloat16)
    low = (table - high.astype(np.float64)).astype(ml_dtypes.bfloat16)
    return high, low


def wave(length, left, right):
    phase = np.outer(left, right) % length
    angle = phase * (2.0 * np.pi / length)
    return np.cos(angle), np.sin(angle)


def make_tables():
    modes = np.arange(M)
    ky = 4 * (modes % 8) + modes // 8
    tables = {}
    cos_y, sin_y = wave(Y, ky, np.arange(Y))
    high, low = halves(np.concatenate([cos_y, -sin_y]))
    tables["yf"] = np.concatenate([high, low])
    high, low = halves(GRAD * np.concatenate([cos_y, -sin_y]))
    tables["yg"] = np.concatenate(
        [np.concatenate([high, high], 1), np.concatenate([low, np.zeros_like(low)], 1)]
    )
    cos_x, sin_x = wave(X, modes, np.arange(X))
    high, low = halves(
        np.concatenate(
            [np.concatenate([cos_x, sin_x], 1), np.concatenate([-sin_x, cos_x], 1)]
        )
    )
    tables["xf"] = np.concatenate([high, low])
    high, low = halves(
        np.concatenate(
            [np.concatenate([cos_y, sin_y], 1), np.concatenate([-sin_y, cos_y], 1)]
        )
    )
    zero = np.zeros_like(low)
    tables["yi"] = np.stack(
        [np.concatenate([high, high, low, zero]), np.concatenate([high, high, zero, low])]
    )
    for name, scale in (("xi", 0.5 * SCALE), ("xj", 1.0)):
        high, low = halves(scale * np.concatenate([cos_x, -sin_x]).T)
        tables[name] = np.concatenate([high, high, low], 1)
    cos_z, sin_z = wave(Z, np.arange(Z), np.tile(modes, 4))
    tables["zf"] = np.stack(
        halves(
            np.concatenate(
                [np.concatenate([cos_z, -sin_z], 1), np.concatenate([sin_z, cos_z], 1)]
            )
        )
    )
    tables["zi"] = np.stack(halves(np.concatenate([cos_z, sin_z], 1)))
    return tables


TABLES = make_tables()
NAMES = ("yf", "yg", "xf", "xi", "zf", "zi", "yi", "xj")


def dot(a, b):
    return lax.dot_general(a, b, (((1,), (0,)), ((), ())), preferred_element_type=F32)


def dot_nt(a, b, precision=None):
    return lax.dot_general(
        a, b, (((1,), (1,)), ((), ())), preferred_element_type=F32, precision=precision
    )


def split(values):
    high = values.astype(BF)
    return high, (values - high.astype(F32)).astype(BF)


def side(arrays):
    return jnp.concatenate(arrays, axis=1)


def stack(arrays):
    return jnp.concatenate(arrays, axis=0)


def forward_x(sections, xf, out, group, zp):
    rows = []
    for zz in range(2):
        at = slice(zz * X, (zz + 1) * X)
        rows += [side([section[:M, at], section[M:, at]]) for section in sections]
    high, low = split(stack(rows))
    wide = dot_nt(xf[...], high)
    total = wide[:64] + wide[64:] + dot_nt(xf[0:64, :], low)
    flat = out.reshape(GROUPS * 64, 128)
    for zz in range(2):
        for part in range(2):
            first = group * 16 + part * ZL + 2 * zp + zz
            flat[pl.ds(first, M, stride=64), :] = total[
                part * M : (part + 1) * M, zz * 128 : (zz + 1) * 128
            ]


def field_forward(field, yf, xf, out, group):
    @pl.loop(0, ZL // 2)
    def _(zp):
        sections = []
        for k in range(4):
            c = group * 4 + k
            both = dot_nt(yf[...], stack([field[2 * zp, c], field[2 * zp + 1, c]]))
            sections.append(both[:64] + both[64:])
        forward_x(sections, xf, out, group, zp)


def depth_forward(planes, zf, group):
    halves_in = []
    for part in range(2):
        turned = planes[:, group, part * ZL : (part + 1) * ZL, :].reshape(Z, 128).T
        halves_in.append(
            stack([turned[k * 32 + j * 8 : k * 32 + j * 8 + 8] for j in range(4) for k in range(4)])
        )
    high, low = split(side(halves_in))
    wide = dot(high, zf[0]) + dot(low, zf[0]) + dot(high, zf[1])
    which = lax.broadcasted_iota(jnp.int32, (32, 256), 1) // 32 % 4
    total = wide[:32]
    for j in range(1, 4):
        total = jnp.where(which == j, wide[j * 32 : (j + 1) * 32], total)
    return total


def depth_inverse(spectrum, zi, out, group):
    lane = lax.broadcasted_iota(jnp.int32, (8, 128), 1) // 32
    right = []
    for k in range(4):
        at = pl.ds(group * 4 + k, 8, stride=C)
        real_in = spectrum[0, at, :]
        imag_in = spectrum[1, at, :]
        real_in = stack([jnp.where(lane == j, real_in, 0.0) for j in range(4)])
        imag_in = stack([jnp.where(lane == j, imag_in, 0.0) for j in range(4)])
        right += [side([real_in, -imag_in]), side([imag_in, real_in])]
    high, low = split(stack(right))
    total = dot_nt(zi[0], high) + dot_nt(zi[0], low) + dot_nt(zi[1], high)
    for pair in range(2):
        out[:, group, pair * ZL : (pair + 1) * ZL, :] = total[
            :, pair * 128 : (pair + 1) * 128
        ].reshape(GROUPS, ZL, 128)


def mix(spec, weight, mixed, group):
    @pl.loop(0, 8)
    def _(g):
        lanes = pl.ds(pl.multiple_of(g * 128, 128), 128)
        at = pl.ds(pl.multiple_of(g * C, C), C)
        real_out = mixed[0, at, :]
        imag_out = mixed[1, at, :]
        for k in range(4):
            c = group * 4 + k
            real_in = spec[0, pl.ds(c * 8 + g, 1), :]
            imag_in = spec[1, pl.ds(c * 8 + g, 1), :]
            wr = weight[0, c, :, lanes].astype(F32)
            wi = weight[1, c, :, lanes].astype(F32)
            real_out += real_in * wr - imag_in * wi
            imag_out += real_in * wi + imag_in * wr
        mixed[0, at, :] = real_out
        mixed[1, at, :] = imag_out


def mix_adjoint(spec, weight, mixed, group):
    @pl.loop(0, 8)
    def _(g):
        lanes = pl.ds(pl.multiple_of(g * 128, 128), 128)
        real_in = spec[0, pl.ds(g, C, stride=8), :]
        imag_in = spec[1, pl.ds(g, C, stride=8), :]
        for k in range(4):
            c = group * 4 + k
            wr = weight[0, c, :, lanes].astype(F32)
            wi = weight[1, c, :, lanes].astype(F32)
            at = pl.ds(g * C + c, 1)
            mixed[0, at, :] = jnp.sum(real_in * wr + imag_in * wi, axis=0, keepdims=True)
            mixed[1, at, :] = jnp.sum(imag_in * wr - real_in * wi, axis=0, keepdims=True)


def weight_grad(spec, grad, out):
    factor = math.sqrt(MODES / CELLS)

    @pl.loop(0, 8)
    def _(g):
        lanes = pl.ds(pl.multiple_of(g * 128, 128), 128)
        grads = [
            [grad[s, part, pl.ds(g, C, stride=8), :] * factor for part in range(2)]
            for s in range(SAMPLES)
        ]
        for c in range(C):
            real_out = jnp.zeros((C, 128), F32)
            imag_out = jnp.zeros((C, 128), F32)
            for s in range(SAMPLES):
                ur = spec[s, 0, pl.ds(c * 8 + g, 1), :]
                ui = spec[s, 1, pl.ds(c * 8 + g, 1), :]
                gr, gi = grads[s]
                real_out += ur * gr + ui * gi
                imag_out += ur * gi - ui * gr
            out[0, c, :, lanes] = real_out
            out[1, c, :, lanes] = imag_out


def inverse_y(planes, yi, middle, group):
    flat = planes.reshape(GROUPS * 64, 128)
    lane = lax.broadcasted_iota(jnp.int32, (256, 128), 1)
    for pair in range(2):
        values = stack(
            [flat[pl.ds(group * 16 + pair * ZL + z, M, stride=64), :] for z in range(ZL)]
        )
        high = values.astype(BF)
        wide = high.astype(F32)
        turned = pltpu.roll(values - wide, 64, 1)
        even = jnp.where(lane < 64, wide, turned).astype(BF)
        odd = jnp.where(lane < 64, turned, wide).astype(BF)
        middle[2 * pair] = dot(side([even, high]), yi[0])
        middle[2 * pair + 1] = dot(side([odd, high]), yi[1])


def inverse_x(middle, table, zp, k):
    first = middle[k, pl.ds(pl.multiple_of(2 * zp * M, M), M), :]
    second = middle[k, pl.ds(pl.multiple_of((2 * zp + 1) * M, M), M), :]
    high, low = split(
        stack([side([first[:, :Y], second[:, :Y]]), side([first[:, Y:], second[:, Y:]])])
    )
    return dot(table[...], stack([high, low, high]))


def cells_of(ref, zp, rows):
    return side([ref[2 * zp + zz, :, rows, :].reshape(C * 16, Y) for zz in range(2)])


def spread(ref, lefts, local, scale):
    @pl.loop(0, X // 16)
    def _(xb):
        rows = pl.ds(pl.multiple_of(xb * 16, 16), 16)
        for zp in range(ZL // 2):
            total = None
            for source in lefts:
                term = dot(ref[...], cells_of(source, zp, rows))
                total = term if total is None else total + term
            for zz in range(2):
                local[2 * zp + zz, :, rows, :] = (
                    total[:, zz * Y : (zz + 1) * Y] * scale
                ).reshape(C, 16, Y)


def step_kernel(*refs):
    fields, cotangent, weights, pointwise = refs[:4]
    sources = dict(zip(NAMES, refs[4 : 4 + len(NAMES)]))
    refs = refs[4 + len(NAMES) :]
    act_out, grad_in, point_out, spec_grad, local, recv_d, yi, xj = refs[:8]
    act = act_out.at[0]
    refs = refs[8:]
    tables = dict(zip(NAMES, refs[: len(NAMES) - 2]))
    tables.update(yi=yi, xj=xj)
    refs = refs[len(NAMES) - 2 :]
    (
        field, cot, weight, high_g, low_g,
        send_a, recv_a, send_b, recv_b, send_c, recv_c, send_d,
        specs, grads, mixed, middle, spread_out, spread_in, point_acc,
        point_z, point_y, point_x, pre,
        load_sem, send_sem, recv_sem, small_send, small_recv,
    ) = refs
    me = lax.axis_index("gz")
    dp = lax.axis_index("dp")

    barrier = pltpu.get_barrier_semaphore()

    @pl.loop(1, GROUPS)
    def _(k):
        pl.semaphore_signal(
            barrier, inc=1, device_id=(dp, lax.rem(me + k, GROUPS)), device_id_type=MESH
        )

    for k in range(1, SAMPLES):
        pl.semaphore_signal(
            barrier, inc=1, device_id=(lax.rem(dp + k, SAMPLES), me), device_id_type=MESH
        )

    def channels(group):
        return pl.ds(group * 4, 4)

    def field_load(group):
        return pltpu.make_async_copy(
            fields.at[0, :, channels(group)], field.at[:, channels(group)], load_sem.at[group]
        )

    def cot_load(group):
        return pltpu.make_async_copy(
            cotangent.at[0, :, channels(group)], cot.at[:, channels(group)], load_sem.at[4 + group]
        )

    def table_load(name):
        return pltpu.make_async_copy(
            sources[name], tables[name], load_sem.at[8 + NAMES.index(name)]
        )

    weight_load = pltpu.make_async_copy(weights, weight, load_sem.at[16])
    for name in ("yf", "xf"):
        table_load(name).start()
    for group in range(4):
        field_load(group).start()
    for name in NAMES:
        if name not in ("yf", "xf"):
            table_load(name).start()
    weight_load.start()
    for group in range(4):
        cot_load(group).start()

    def send(index, group, source, target):
        @pl.loop(1, GROUPS)
        def _(k):
            peer = lax.rem(me + k, GROUPS)
            pltpu.make_async_remote_copy(
                src_ref=source.at[peer, group],
                dst_ref=target.at[me, group],
                send_sem=send_sem.at[index, group],
                recv_sem=recv_sem.at[index, group],
                device_id=(dp, peer),
                device_id_type=MESH,
            ).start()

        target[me, group] = source[me, group]

    def wait_planes(sem, index, group, buffer):
        part = buffer.at[pl.ds(0, GROUPS - 1), group]
        pltpu.make_async_copy(part, part, sem.at[index, group]).wait()

    def small(index, buffer, slot, count, place):
        for k in range(1, count):
            pltpu.make_async_remote_copy(
                src_ref=buffer.at[slot],
                dst_ref=buffer.at[slot],
                send_sem=small_send.at[index],
                recv_sem=small_recv.at[index],
                device_id=place(k),
                device_id_type=MESH,
            ).start()

    def small_wait(sem, index, buffer, count):
        part = buffer.at[pl.ds(0, count - 1)]
        pltpu.make_async_copy(part, part, sem.at[index]).wait()

    def along_dp(k):
        return lax.rem(dp + k, SAMPLES), me

    def along_z(k):
        return dp, me // 8 * 8 + lax.rem(me + k, 8)

    def along_y(k):
        return dp, lax.rem(me + 8 * k, GROUPS)

    for name in ("yf", "xf"):
        table_load(name).wait()

    field_load(0).wait()
    field_forward(field, tables["yf"], tables["xf"], send_a, 0)
    pl.semaphore_wait(barrier, GROUPS - 1 + SAMPLES - 1)
    send(0, 0, send_a, recv_a)

    @pl.loop(1, 4)
    def _(group):
        field_load(group).wait()
        field_forward(field, tables["yf"], tables["xf"], send_a, group)
        send(0, group, send_a, recv_a)

    place = lax.broadcasted_iota(jnp.int32, (256, C), 0) // 16
    one_hot = (place == lax.broadcasted_iota(jnp.int32, (256, C), 1)).astype(F32).astype(BF)
    same = (
        lax.broadcasted_iota(jnp.int32, (256, 256), 0) % 16
        == lax.broadcasted_iota(jnp.int32, (256, 256), 1) % 16
    )
    for left, target in (
        (dot_nt(one_hot, pointwise[...]), spread_out),
        (dot(one_hot, pointwise[...]), spread_in),
    ):
        target[...] = jnp.where(same, dot_nt(left.astype(BF), one_hot), 0.0).astype(BF)
    spread(spread_out, (field,), local, 0.5)
    for name in NAMES:
        if name not in ("yf", "xf"):
            table_load(name).wait()
    weight_load.wait()

    def keep_spectrum(target, group, spec):
        rows = pl.ds(pl.multiple_of(group * 32, 32), 32)
        target[dp, 0, rows, :] = spec[:, :128]
        target[dp, 1, rows, :] = spec[:, 128:]

    mixed[...] = jnp.zeros_like(mixed)

    @pl.loop(0, 4)
    def _(group):
        wait_planes(recv_sem, 0, group, recv_a)
        keep_spectrum(specs, group, depth_forward(recv_a, tables["zf"], group))
        mix(specs.at[dp], weight, mixed, group)

    @pl.loop(0, 4)
    def _(group):
        depth_inverse(mixed, tables["zi"], send_b, group)
        send(1, group, send_b, recv_b)

    small(0, specs, dp, SAMPLES, along_dp)

    @pl.loop(0, 4)
    def _(group):
        wait_planes(recv_sem, 1, group, recv_b)
        inverse_y(recv_b, tables["yi"], middle, group)
        cot_load(group).wait()

        for zp in range(ZL // 2 + 2):
            sections = []
            for k in range(4):
                o = group * 4 + k
                if zp < ZL // 2:
                    both = inverse_x(middle, tables["xi"], zp, k)
                    for zz in range(2):
                        pre[zp % 2, k, zz] = both[:, zz * Y : (zz + 1) * Y]
                if 1 <= zp <= ZL // 2:
                    for zz in range(2):
                        z = 2 * (zp - 1) + zz
                        values = pre[(zp - 1) % 2, k, zz] + local[z, o]
                        inner = values * (2.0 * K0 + 8.0 * K1 * (values * values))
                        wave_t = jnp.tanh(inner)
                        twice = 1.0 + wave_t
                        act[z, o] = (values * twice).astype(BF)
                        slope = 1.0 / 3.0 + (inner - (4.0 / 3.0 * K0) * values) * (1.0 - wave_t)
                        high, low = split(cot[z, o].astype(F32) * twice * slope)
                        high_g[z, o] = high
                        low_g[z, o] = low
                if 2 <= zp:
                    right = [
                        side([high_g[2 * (zp - 2) + zz, o], low_g[2 * (zp - 2) + zz, o]])
                        for zz in range(2)
                    ]
                    wide = dot_nt(tables["yg"][...], stack(right))
                    sections.append(wide[:64] + wide[64:])
            if 2 <= zp:
                forward_x(sections, tables["xf"], send_c, group, zp - 2)

        send(2, group, send_c, recv_c)

    point_acc[...] = jnp.zeros_like(point_acc)

    def point_half(first):
        @pl.loop(first, first + 4)
        def _(xb):
            rows = pl.ds(pl.multiple_of(xb * 16, 16), 16)
            total = None
            for zp in range(ZL // 2):
                cells = cells_of(field, zp, rows)
                term = dot_nt(cells_of(high_g, zp, rows), cells)
                term += dot_nt(cells_of(low_g, zp, rows), cells)
                total = term if total is None else total + term
            point_acc[...] += total

    point_half(0)
    point_half(4)
    kept = jnp.where(same, point_acc[...], 0.0).reshape(C, 16, 256).sum(axis=1)
    groups = lax.broadcasted_iota(jnp.int32, (C, 256), 1) // 16
    picks = (groups == lax.broadcasted_iota(jnp.int32, (C, 256), 0)).astype(F32)
    kept = stack([kept, jnp.zeros((128 - C, 256), F32)])
    z_slot = lax.rem(me, 8)
    y_slot = me // 8
    point_z[z_slot] = dot_nt(picks, kept, lax.Precision.HIGHEST)
    small(1, point_z, z_slot, 8, along_z)


    @pl.loop(0, 4)
    def _(group):
        wait_planes(recv_sem, 2, group, recv_c)
        keep_spectrum(grads, group, depth_forward(recv_c, tables["zf"], group) * SCALE)

    small(2, grads, dp, SAMPLES, along_dp)

    def adjoint_group(group):
        mix_adjoint(grads.at[dp], weight, mixed, group)
        depth_inverse(mixed, tables["zi"], send_d, group)
        send(3, group, send_d, recv_d)

    pl.loop(0, 4)(adjoint_group)
    spread(spread_in, (high_g, low_g), local, GRAD)
    small_wait(small_recv, 1, point_z, 8)
    point_x[dp] = jnp.sum(point_z[...], axis=0)
    small(4, point_x, dp, SAMPLES, along_dp)
    small_wait(small_recv, 0, specs, SAMPLES)
    small_wait(small_recv, 2, grads, SAMPLES)
    weight_grad(specs, grads, spec_grad)
    small_wait(small_recv, 4, point_x, SAMPLES)
    point_y[y_slot] = jnp.sum(point_x[...], axis=0)
    small(3, point_y, y_slot, 4, along_y)

    @pl.loop(0, 3)
    def _(group):
        wait_planes(recv_sem, 3, group, recv_d)
        input_grad(recv_d, tables["yi"], tables["xj"], middle, local, grad_in, group, group)

    wait_planes(recv_sem, 3, 3, recv_d)
    small_wait(small_recv, 3, point_y, 4)
    total = jnp.sum(point_y[...], axis=0)
    point_out[...] = total[:, 0:C] * (GRAD / math.sqrt(CELLS))

    for index, buffer in enumerate((send_a, send_b, send_c, send_d)):
        @pl.loop(0, 4)
        def _(group):
            wait_planes(send_sem, index, group, buffer)

    for index, (buffer, count) in enumerate(
        ((specs, 4), (point_z, 8), (grads, 4), (point_y, 4), (point_x, 4))
    ):
        small_wait(small_send, index, buffer, count)


def input_grad(planes, yi, xj, middle, local, out, group, place):
    inverse_y(planes, yi, middle, group)

    @pl.loop(0, ZL // 2)
    def _(zp):
        for k in range(4):
            both = inverse_x(middle, xj, zp, k)
            for zz in range(2):
                z = 2 * zp + zz
                values = both[:, zz * Y : (zz + 1) * Y] + local[z, group * 4 + k]
                out[z, place * 4 + k] = values.astype(BF)


def store_kernel(
    act, grad_in, point, spec_grad, local, planes, yi, xj,
    act_out, grad_out, point_out, spec_grad_out, middle, last, sems,
):
    copies = [
        pltpu.make_async_copy(act, act_out, sems.at[0]),
        pltpu.make_async_copy(grad_in, grad_out.at[0, :, 0:12], sems.at[1]),
        pltpu.make_async_copy(point, point_out, sems.at[2]),
        pltpu.make_async_copy(spec_grad, spec_grad_out, sems.at[3]),
    ]
    for copy in copies:
        copy.start()
    input_grad(planes, yi, xj, middle, local, last, 3, 0)
    copies.append(pltpu.make_async_copy(last, grad_out.at[0, :, 12:16], sems.at[4]))
    copies[4].start()
    for copy in copies:
        copy.wait()


def shards(fields, cotangent, spectral_weight, pointwise_weight):
    tables = [jnp.asarray(TABLES[name]) for name in NAMES]
    grid_shape = (ZL, C, X, Y)
    planes = pltpu.VMEM((GROUPS, 4, 16, 128), F32)
    scratch = [pltpu.VMEM(table.shape, BF) for table in tables[:-2]]
    scratch += [pltpu.VMEM(grid_shape, BF)] * 2
    scratch += [pltpu.VMEM((2, C, C, M * M), BF)]
    scratch += [pltpu.VMEM(grid_shape, BF)] * 2
    scratch += [planes] * 7
    scratch += [pltpu.VMEM((SAMPLES, 2, 128, 128), F32)] * 2
    scratch += [
        pltpu.VMEM((2, 128, 128), F32),
        pltpu.VMEM((4, 256, 256), F32),
        pltpu.VMEM((256, 256), BF),
        pltpu.VMEM((256, 256), BF),
        pltpu.VMEM((256, 256), F32),
        pltpu.VMEM((8, C, 128), F32),
        pltpu.VMEM((4, C, 128), F32),
        pltpu.VMEM((SAMPLES, C, 128), F32),
        pltpu.VMEM((2, 4, 2, X, Y), F32),
        pltpu.SemaphoreType.DMA((17,)),
        pltpu.SemaphoreType.DMA((4, 4)),
        pltpu.SemaphoreType.DMA((4, 4)),
        pltpu.SemaphoreType.DMA((5,)),
        pltpu.SemaphoreType.DMA((5,)),
    ]
    anywhere = pl.BlockSpec(memory_space=pl.ANY)
    on_chip = pl.BlockSpec(memory_space=pltpu.VMEM)
    shapes = (
        jax.ShapeDtypeStruct((1,) + grid_shape, BF),
        jax.ShapeDtypeStruct((1,) + grid_shape, BF),
        jax.ShapeDtypeStruct((C, C), F32),
        jax.ShapeDtypeStruct((2, C, C, M * M), F32),
    )
    results = pl.pallas_call(
        step_kernel,
        in_specs=[anywhere] * 3 + [on_chip] + [anywhere] * len(tables),
        out_specs=(on_chip,) * 8,
        out_shape=(
            pltpu.VMEM((1,) + grid_shape, BF),
            pltpu.VMEM((ZL, 12, X, Y), BF),
            pltpu.VMEM((C, C), F32),
            pltpu.VMEM((2, C, C, M * M), F32),
            pltpu.VMEM(grid_shape, F32),
            planes,
            pltpu.VMEM(tables[-2].shape, BF),
            pltpu.VMEM(tables[-1].shape, BF),
        ),
        scratch_shapes=scratch,
        compiler_params=pltpu.CompilerParams(
            vmem_limit_bytes=VMEM_LIMIT, collective_id=0, has_side_effects=True
        ),
        name="step",
    )(fields, cotangent, spectral_weight, pointwise_weight, *tables)
    return pl.pallas_call(
        store_kernel,
        in_specs=[on_chip] * 8,
        out_specs=(anywhere,) * 4,
        out_shape=shapes,
        scratch_shapes=[
            pltpu.VMEM((4, 256, 256), F32),
            pltpu.VMEM((ZL, 4, X, Y), BF),
            pltpu.SemaphoreType.DMA((5,)),
        ],
        compiler_params=pltpu.CompilerParams(vmem_limit_bytes=8 * 1024 * 1024),
        name="store",
    )(*results)


def solution(mesh):
    placed = (
        P("dp", "gz", None, None, None),
        P("dp", "gz", None, None, None),
        P(None, None, None, "gz"),
        P(),
    )
    return jax.shard_map(
        shards,
        mesh=mesh,
        in_specs=placed,
        out_specs=(
            P("dp", "gz", None, None, None),
            P("dp", "gz", None, None, None),
            P(),
            P(None, None, None, "gz"),
        ),
        check_vma=False,
    )
```

```python
import math

import jax
import jax.numpy as jnp
import ml_dtypes
import numpy as np
from jax import lax
from jax.experimental import pallas as pl
from jax.experimental.pallas import tpu as pltpu
from jax.sharding import PartitionSpec as P

M = 32
C = 16
ZL = 8
X = 128
Y = 128
Z = 256
GROUPS = 32
SAMPLES = 4
MODES = M * M * M
CELLS = SAMPLES * X * Y * Z
SCALE = 1.0 / math.sqrt(X * Y * Z * MODES)
BF = jnp.bfloat16
F32 = jnp.float32
VMEM_LIMIT = 42 * 1024 * 1024
K0 = math.sqrt(2.0 / math.pi)
K1 = K0 * 0.044715
GRAD = 1.5
MESH = pl.DeviceIdType.MESH


def halves(table):
    high = table.astype(ml_dtypes.bfloat16)
    low = (table - high.astype(np.float64)).astype(ml_dtypes.bfloat16)
    return high, low


def wave(length, left, right):
    phase = np.outer(left, right) % length
    angle = phase * (2.0 * np.pi / length)
    return np.cos(angle), np.sin(angle)


def make_tables():
    modes = np.arange(M)
    ky = 4 * (modes % 8) + modes // 8
    tables = {}
    cos_y, sin_y = wave(Y, ky, np.arange(Y))
    high, low = halves(np.concatenate([cos_y, -sin_y]))
    tables["yf"] = np.concatenate([high, low])
    high, low = halves(GRAD * np.concatenate([cos_y, -sin_y]))
    tables["yg"] = np.concatenate(
        [np.concatenate([high, high], 1), np.concatenate([low, np.zeros_like(low)], 1)]
    )
    cos_x, sin_x = wave(X, modes, np.arange(X))
    high, low = halves(
        np.concatenate(
            [np.concatenate([cos_x, sin_x], 1), np.concatenate([-sin_x, cos_x], 1)]
        )
    )
    tables["xf"] = np.concatenate([high, low])
    high, low = halves(
        np.concatenate(
            [np.concatenate([cos_y, sin_y], 1), np.concatenate([-sin_y, cos_y], 1)]
        )
    )
    zero = np.zeros_like(low)
    tables["yi"] = np.stack(
        [np.concatenate([high, high, low, zero]), np.concatenate([high, high, zero, low])]
    )
    for name, scale in (("xi", 0.5 * SCALE), ("xj", 1.0)):
        high, low = halves(scale * np.concatenate([cos_x, -sin_x]).T)
        tables[name] = np.concatenate([high, high, low], 1)
    cos_z, sin_z = wave(Z, np.arange(Z), np.tile(modes, 4))
    tables["zf"] = np.stack(
        halves(
            np.concatenate(
                [np.concatenate([cos_z, -sin_z], 1), np.concatenate([sin_z, cos_z], 1)]
            )
        )
    )
    tables["zi"] = np.stack(halves(np.concatenate([cos_z, sin_z], 1)))
    return tables


TABLES = make_tables()
NAMES = ("yf", "yg", "xf", "xi", "zf", "zi", "yi", "xj")


def dot(a, b):
    return lax.dot_general(a, b, (((1,), (0,)), ((), ())), preferred_element_type=F32)


def dot_nt(a, b, precision=None):
    return lax.dot_general(
        a, b, (((1,), (1,)), ((), ())), preferred_element_type=F32, precision=precision
    )


def split(values):
    high = values.astype(BF)
    return high, (values - high.astype(F32)).astype(BF)


def side(arrays):
    return jnp.concatenate(arrays, axis=1)


def stack(arrays):
    return jnp.concatenate(arrays, axis=0)


def forward_x(sections, xf, out, group, zp):
    rows = []
    for zz in range(2):
        at = slice(zz * X, (zz + 1) * X)
        rows += [side([section[:M, at], section[M:, at]]) for section in sections]
    high, low = split(stack(rows))
    wide = dot_nt(xf[...], high)
    total = wide[:64] + wide[64:] + dot_nt(xf[0:64, :], low)
    flat = out.reshape(GROUPS * 64, 128)
    for zz in range(2):
        for part in range(2):
            first = group * 16 + part * ZL + 2 * zp + zz
            flat[pl.ds(first, M, stride=64), :] = total[
                part * M : (part + 1) * M, zz * 128 : (zz + 1) * 128
            ]


def field_forward(field, yf, xf, out, group, ready=lambda zp: None):
    @pl.loop(0, ZL // 2)
    def _(zp):
        ready(zp)
        sections = []
        for k in range(4):
            c = group * 4 + k
            both = dot_nt(yf[...], stack([field[2 * zp, c], field[2 * zp + 1, c]]))
            sections.append(both[:64] + both[64:])
        forward_x(sections, xf, out, group, zp)


def depth_forward(planes, zf, group):
    halves_in = []
    for part in range(2):
        turned = planes[:, group, part * ZL : (part + 1) * ZL, :].reshape(Z, 128).T
        halves_in.append(
            stack([turned[k * 32 + j * 8 : k * 32 + j * 8 + 8] for j in range(4) for k in range(4)])
        )
    high, low = split(side(halves_in))
    wide = dot(high, zf[0]) + dot(low, zf[0]) + dot(high, zf[1])
    which = lax.broadcasted_iota(jnp.int32, (32, 256), 1) // 32 % 4
    total = wide[:32]
    for j in range(1, 4):
        total = jnp.where(which == j, wide[j * 32 : (j + 1) * 32], total)
    return total


def depth_inverse(spectrum, zi, out, group):
    lane = lax.broadcasted_iota(jnp.int32, (8, 128), 1) // 32
    right = []
    for k in range(4):
        at = pl.ds(group * 4 + k, 8, stride=C)
        real_in = spectrum[0, at, :]
        imag_in = spectrum[1, at, :]
        real_in = stack([jnp.where(lane == j, real_in, 0.0) for j in range(4)])
        imag_in = stack([jnp.where(lane == j, imag_in, 0.0) for j in range(4)])
        right += [side([real_in, -imag_in]), side([imag_in, real_in])]
    high, low = split(stack(right))
    total = dot_nt(zi[0], high) + dot_nt(zi[0], low) + dot_nt(zi[1], high)
    for pair in range(2):
        out[:, group, pair * ZL : (pair + 1) * ZL, :] = total[
            :, pair * 128 : (pair + 1) * 128
        ].reshape(GROUPS, ZL, 128)


def mix(spec, weight, mixed, group):
    @pl.loop(0, 8)
    def _(g):
        lanes = pl.ds(pl.multiple_of(g * 128, 128), 128)
        at = pl.ds(pl.multiple_of(g * C, C), C)
        real_out = mixed[0, at, :]
        imag_out = mixed[1, at, :]
        for k in range(4):
            c = group * 4 + k
            real_in = spec[0, pl.ds(c * 8 + g, 1), :]
            imag_in = spec[1, pl.ds(c * 8 + g, 1), :]
            wr = weight[0, c, :, lanes].astype(F32)
            wi = weight[1, c, :, lanes].astype(F32)
            real_out += real_in * wr - imag_in * wi
            imag_out += real_in * wi + imag_in * wr
        mixed[0, at, :] = real_out
        mixed[1, at, :] = imag_out


def mix_adjoint(spec, weight, mixed, group):
    @pl.loop(0, 8)
    def _(g):
        lanes = pl.ds(pl.multiple_of(g * 128, 128), 128)
        real_in = spec[0, pl.ds(g, C, stride=8), :]
        imag_in = spec[1, pl.ds(g, C, stride=8), :]
        for k in range(4):
            c = group * 4 + k
            wr = weight[0, c, :, lanes].astype(F32)
            wi = weight[1, c, :, lanes].astype(F32)
            at = pl.ds(g * C + c, 1)
            mixed[0, at, :] = jnp.sum(real_in * wr + imag_in * wi, axis=0, keepdims=True)
            mixed[1, at, :] = jnp.sum(imag_in * wr - real_in * wi, axis=0, keepdims=True)


def weight_grad(spec, grad, out):
    factor = math.sqrt(MODES / CELLS)

    @pl.loop(0, 8)
    def _(g):
        lanes = pl.ds(pl.multiple_of(g * 128, 128), 128)
        grads = [
            [grad[s, part, pl.ds(g, C, stride=8), :] * factor for part in range(2)]
            for s in range(SAMPLES)
        ]
        for c in range(C):
            real_out = jnp.zeros((C, 128), F32)
            imag_out = jnp.zeros((C, 128), F32)
            for s in range(SAMPLES):
                ur = spec[s, 0, pl.ds(c * 8 + g, 1), :]
                ui = spec[s, 1, pl.ds(c * 8 + g, 1), :]
                gr, gi = grads[s]
                real_out += ur * gr + ui * gi
                imag_out += ur * gi - ui * gr
            out[0, c, :, lanes] = real_out
            out[1, c, :, lanes] = imag_out


def inverse_y(planes, yi, middle, group):
    flat = planes.reshape(GROUPS * 64, 128)
    lane = lax.broadcasted_iota(jnp.int32, (256, 128), 1)
    for pair in range(2):
        values = stack(
            [flat[pl.ds(group * 16 + pair * ZL + z, M, stride=64), :] for z in range(ZL)]
        )
        high = values.astype(BF)
        wide = high.astype(F32)
        turned = pltpu.roll(values - wide, 64, 1)
        even = jnp.where(lane < 64, wide, turned).astype(BF)
        odd = jnp.where(lane < 64, turned, wide).astype(BF)
        middle[2 * pair] = dot(side([even, high]), yi[0])
        middle[2 * pair + 1] = dot(side([odd, high]), yi[1])


def inverse_x(middle, table, zp, k):
    first = middle[k, pl.ds(pl.multiple_of(2 * zp * M, M), M), :]
    second = middle[k, pl.ds(pl.multiple_of((2 * zp + 1) * M, M), M), :]
    high, low = split(
        stack([side([first[:, :Y], second[:, :Y]]), side([first[:, Y:], second[:, Y:]])])
    )
    return dot(table[...], stack([high, low, high]))


def cells_of(ref, zp, rows):
    return side([ref[2 * zp + zz, :, rows, :].reshape(C * 16, Y) for zz in range(2)])


def spread(ref, lefts, local, scale):
    @pl.loop(0, X // 16)
    def _(xb):
        rows = pl.ds(pl.multiple_of(xb * 16, 16), 16)
        for zp in range(ZL // 2):
            total = None
            for source in lefts:
                term = dot(ref[...], cells_of(source, zp, rows))
                total = term if total is None else total + term
            for zz in range(2):
                local[2 * zp + zz, :, rows, :] = (
                    total[:, zz * Y : (zz + 1) * Y] * scale
                ).reshape(C, 16, Y)


def step_kernel(*refs):
    fields, cotangent, weights, pointwise = refs[:4]
    sources = dict(zip(NAMES, refs[4 : 4 + len(NAMES)]))
    refs = refs[4 + len(NAMES) :]
    act_out, grad_in, point_out, spec_grad, local, recv_d, yi, xj = refs[:8]
    act = act_out.at[0]
    refs = refs[8:]
    tables = dict(zip(NAMES, refs[: len(NAMES) - 2]))
    tables.update(yi=yi, xj=xj)
    refs = refs[len(NAMES) - 2 :]
    (
        field, cot, weight, high_g, low_g,
        send_a, recv_a, send_b, recv_b, send_c, recv_c, send_d,
        specs, grads, mixed, middle, spread_out, spread_in, point_acc,
        point_z, point_y, point_x, pre,
        load_sem, first_sem, send_sem, recv_sem, small_send, small_recv,
    ) = refs
    me = lax.axis_index("gz")
    dp = lax.axis_index("dp")

    barrier = pltpu.get_barrier_semaphore()

    @pl.loop(1, GROUPS)
    def _(k):
        pl.semaphore_signal(
            barrier, inc=1, device_id=(dp, lax.rem(me + k, GROUPS)), device_id_type=MESH
        )

    for k in range(1, SAMPLES):
        pl.semaphore_signal(
            barrier, inc=1, device_id=(lax.rem(dp + k, SAMPLES), me), device_id_type=MESH
        )

    def channels(group):
        return pl.ds(group * 4, 4)

    def field_load(group):
        return pltpu.make_async_copy(
            fields.at[0, :, channels(group)], field.at[:, channels(group)], load_sem.at[group]
        )

    def cot_load(group):
        return pltpu.make_async_copy(
            cotangent.at[0, :, channels(group)], cot.at[:, channels(group)], load_sem.at[4 + group]
        )

    def table_load(name):
        return pltpu.make_async_copy(
            sources[name], tables[name], load_sem.at[8 + NAMES.index(name)]
        )

    weight_load = pltpu.make_async_copy(weights, weight, load_sem.at[16])
    for name in ("yf", "xf"):
        table_load(name).start()
    def first_load(zp):
        planes = pl.ds(2 * zp, 2)
        return pltpu.make_async_copy(
            fields.at[0, planes, 0:4], field.at[planes, 0:4], first_sem.at[zp]
        )

    for zp in range(ZL // 2):
        first_load(zp).start()
    for group in range(1, 4):
        field_load(group).start()
    for name in NAMES:
        if name not in ("yf", "xf"):
            table_load(name).start()
    weight_load.start()
    for group in range(4):
        cot_load(group).start()

    def send(index, group, source, target):
        @pl.loop(1, GROUPS)
        def _(k):
            peer = lax.rem(me + k, GROUPS)
            pltpu.make_async_remote_copy(
                src_ref=source.at[peer, group],
                dst_ref=target.at[me, group],
                send_sem=send_sem.at[index, group],
                recv_sem=recv_sem.at[index, group],
                device_id=(dp, peer),
                device_id_type=MESH,
            ).start()

        target[me, group] = source[me, group]

    def wait_planes(sem, index, group, buffer):
        part = buffer.at[pl.ds(0, GROUPS - 1), group]
        pltpu.make_async_copy(part, part, sem.at[index, group]).wait()

    def small(index, buffer, slot, count, place):
        for k in range(1, count):
            pltpu.make_async_remote_copy(
                src_ref=buffer.at[slot],
                dst_ref=buffer.at[slot],
                send_sem=small_send.at[index],
                recv_sem=small_recv.at[index],
                device_id=place(k),
                device_id_type=MESH,
            ).start()

    def small_wait(sem, index, buffer, count):
        part = buffer.at[pl.ds(0, count - 1)]
        pltpu.make_async_copy(part, part, sem.at[index]).wait()

    def along_dp(k):
        return lax.rem(dp + k, SAMPLES), me

    def along_z(k):
        return dp, me // 8 * 8 + lax.rem(me + k, 8)

    def along_y(k):
        return dp, lax.rem(me + 8 * k, GROUPS)

    for name in ("yf", "xf"):
        table_load(name).wait()

    field_forward(
        field, tables["yf"], tables["xf"], send_a, 0, lambda zp: first_load(zp).wait()
    )
    pl.semaphore_wait(barrier, GROUPS - 1 + SAMPLES - 1)
    send(0, 0, send_a, recv_a)

    @pl.loop(1, 4)
    def _(group):
        field_load(group).wait()
        field_forward(field, tables["yf"], tables["xf"], send_a, group)
        send(0, group, send_a, recv_a)

    place = lax.broadcasted_iota(jnp.int32, (256, C), 0) // 16
    one_hot = (place == lax.broadcasted_iota(jnp.int32, (256, C), 1)).astype(F32).astype(BF)
    same = (
        lax.broadcasted_iota(jnp.int32, (256, 256), 0) % 16
        == lax.broadcasted_iota(jnp.int32, (256, 256), 1) % 16
    )
    for left, target in (
        (dot_nt(one_hot, pointwise[...]), spread_out),
        (dot(one_hot, pointwise[...]), spread_in),
    ):
        target[...] = jnp.where(same, dot_nt(left.astype(BF), one_hot), 0.0).astype(BF)
    spread(spread_out, (field,), local, 0.5)
    for name in NAMES:
        if name not in ("yf", "xf"):
            table_load(name).wait()
    weight_load.wait()

    def keep_spectrum(target, group, spec):
        rows = pl.ds(pl.multiple_of(group * 32, 32), 32)
        target[dp, 0, rows, :] = spec[:, :128]
        target[dp, 1, rows, :] = spec[:, 128:]

    mixed[...] = jnp.zeros_like(mixed)

    @pl.loop(0, 4)
    def _(group):
        wait_planes(recv_sem, 0, group, recv_a)
        keep_spectrum(specs, group, depth_forward(recv_a, tables["zf"], group))
        mix(specs.at[dp], weight, mixed, group)

    @pl.loop(0, 4)
    def _(group):
        depth_inverse(mixed, tables["zi"], send_b, group)
        send(1, group, send_b, recv_b)

    small(0, specs, dp, SAMPLES, along_dp)

    @pl.loop(0, 4)
    def _(group):
        wait_planes(recv_sem, 1, group, recv_b)
        inverse_y(recv_b, tables["yi"], middle, group)
        cot_load(group).wait()

        for zp in range(ZL // 2 + 2):
            sections = []
            for k in range(4):
                o = group * 4 + k
                if zp < ZL // 2:
                    both = inverse_x(middle, tables["xi"], zp, k)
                    for zz in range(2):
                        pre[zp % 2, k, zz] = both[:, zz * Y : (zz + 1) * Y]
                if 1 <= zp <= ZL // 2:
                    for zz in range(2):
                        z = 2 * (zp - 1) + zz
                        values = pre[(zp - 1) % 2, k, zz] + local[z, o]
                        inner = values * (2.0 * K0 + 8.0 * K1 * (values * values))
                        wave_t = jnp.tanh(inner)
                        twice = 1.0 + wave_t
                        act[z, o] = (values * twice).astype(BF)
                        slope = 1.0 / 3.0 + (inner - (4.0 / 3.0 * K0) * values) * (1.0 - wave_t)
                        high, low = split(cot[z, o].astype(F32) * twice * slope)
                        high_g[z, o] = high
                        low_g[z, o] = low
                if 2 <= zp:
                    right = [
                        side([high_g[2 * (zp - 2) + zz, o], low_g[2 * (zp - 2) + zz, o]])
                        for zz in range(2)
                    ]
                    wide = dot_nt(tables["yg"][...], stack(right))
                    sections.append(wide[:64] + wide[64:])
            if 2 <= zp:
                forward_x(sections, tables["xf"], send_c, group, zp - 2)

        send(2, group, send_c, recv_c)

    point_acc[...] = jnp.zeros_like(point_acc)

    def point_half(first):
        @pl.loop(first, first + 4)
        def _(xb):
            rows = pl.ds(pl.multiple_of(xb * 16, 16), 16)
            total = None
            for zp in range(ZL // 2):
                cells = cells_of(field, zp, rows)
                term = dot_nt(cells_of(high_g, zp, rows), cells)
                term += dot_nt(cells_of(low_g, zp, rows), cells)
                total = term if total is None else total + term
            point_acc[...] += total

    point_half(0)
    point_half(4)
    kept = jnp.where(same, point_acc[...], 0.0).reshape(C, 16, 256).sum(axis=1)
    groups = lax.broadcasted_iota(jnp.int32, (C, 256), 1) // 16
    picks = (groups == lax.broadcasted_iota(jnp.int32, (C, 256), 0)).astype(F32)
    kept = stack([kept, jnp.zeros((128 - C, 256), F32)])
    z_slot = lax.rem(me, 8)
    y_slot = me // 8
    point_z[z_slot] = dot_nt(picks, kept, lax.Precision.HIGHEST)
    small(1, point_z, z_slot, 8, along_z)


    @pl.loop(0, 4)
    def _(group):
        wait_planes(recv_sem, 2, group, recv_c)
        keep_spectrum(grads, group, depth_forward(recv_c, tables["zf"], group) * SCALE)

    small(2, grads, dp, SAMPLES, along_dp)

    def adjoint_group(group):
        mix_adjoint(grads.at[dp], weight, mixed, group)
        depth_inverse(mixed, tables["zi"], send_d, group)
        send(3, group, send_d, recv_d)

    pl.loop(0, 4)(adjoint_group)
    spread(spread_in, (high_g, low_g), local, GRAD)
    small_wait(small_recv, 1, point_z, 8)
    point_x[dp] = jnp.sum(point_z[...], axis=0)
    small(4, point_x, dp, SAMPLES, along_dp)
    small_wait(small_recv, 0, specs, SAMPLES)
    small_wait(small_recv, 2, grads, SAMPLES)
    weight_grad(specs, grads, spec_grad)
    small_wait(small_recv, 4, point_x, SAMPLES)
    point_y[y_slot] = jnp.sum(point_x[...], axis=0)
    small(3, point_y, y_slot, 4, along_y)

    @pl.loop(0, 3)
    def _(group):
        wait_planes(recv_sem, 3, group, recv_d)
        input_grad(recv_d, tables["yi"], tables["xj"], middle, local, grad_in, group, group)

    wait_planes(recv_sem, 3, 3, recv_d)
    small_wait(small_recv, 3, point_y, 4)
    total = jnp.sum(point_y[...], axis=0)
    point_out[...] = total[:, 0:C] * (GRAD / math.sqrt(CELLS))

    for index, buffer in enumerate((send_a, send_b, send_c, send_d)):
        @pl.loop(0, 4)
        def _(group):
            wait_planes(send_sem, index, group, buffer)

    for index, (buffer, count) in enumerate(
        ((specs, 4), (point_z, 8), (grads, 4), (point_y, 4), (point_x, 4))
    ):
        small_wait(small_send, index, buffer, count)


def input_grad(planes, yi, xj, middle, local, out, group, place):
    inverse_y(planes, yi, middle, group)

    @pl.loop(0, ZL // 2)
    def _(zp):
        for k in range(4):
            both = inverse_x(middle, xj, zp, k)
            for zz in range(2):
                z = 2 * zp + zz
                values = both[:, zz * Y : (zz + 1) * Y] + local[z, group * 4 + k]
                out[z, place * 4 + k] = values.astype(BF)


def store_kernel(
    act, grad_in, point, spec_grad, local, planes, yi, xj,
    act_out, grad_out, point_out, spec_grad_out, middle, last, sems,
):
    copies = [
        pltpu.make_async_copy(act, act_out, sems.at[0]),
        pltpu.make_async_copy(grad_in, grad_out.at[0, :, 0:12], sems.at[1]),
        pltpu.make_async_copy(point, point_out, sems.at[2]),
        pltpu.make_async_copy(spec_grad, spec_grad_out, sems.at[3]),
    ]
    for copy in copies:
        copy.start()
    input_grad(planes, yi, xj, middle, local, last, 3, 0)
    copies.append(pltpu.make_async_copy(last, grad_out.at[0, :, 12:16], sems.at[4]))
    copies[4].start()
    for copy in copies:
        copy.wait()


def shards(fields, cotangent, spectral_weight, pointwise_weight):
    tables = [jnp.asarray(TABLES[name]) for name in NAMES]
    grid_shape = (ZL, C, X, Y)
    planes = pltpu.VMEM((GROUPS, 4, 16, 128), F32)
    scratch = [pltpu.VMEM(table.shape, BF) for table in tables[:-2]]
    scratch += [pltpu.VMEM(grid_shape, BF)] * 2
    scratch += [pltpu.VMEM((2, C, C, M * M), BF)]
    scratch += [pltpu.VMEM(grid_shape, BF)] * 2
    scratch += [planes] * 7
    scratch += [pltpu.VMEM((SAMPLES + 1, 2, 128, 128), F32)] * 2
    scratch += [
        pltpu.VMEM((3, 128, 128), F32),
        pltpu.VMEM((4, 256, 256), F32),
        pltpu.VMEM((256, 256), BF),
        pltpu.VMEM((256, 256), BF),
        pltpu.VMEM((256, 256), F32),
        pltpu.VMEM((8, C, 128), F32),
        pltpu.VMEM((4, C, 128), F32),
        pltpu.VMEM((SAMPLES, C, 128), F32),
        pltpu.VMEM((2, 4, 2, X, Y), F32),
        pltpu.SemaphoreType.DMA((17,)),
        pltpu.SemaphoreType.DMA((4,)),
        pltpu.SemaphoreType.DMA((4, 4)),
        pltpu.SemaphoreType.DMA((4, 4)),
        pltpu.SemaphoreType.DMA((5,)),
        pltpu.SemaphoreType.DMA((5,)),
    ]
    anywhere = pl.BlockSpec(memory_space=pl.ANY)
    on_chip = pl.BlockSpec(memory_space=pltpu.VMEM)
    shapes = (
        jax.ShapeDtypeStruct((1,) + grid_shape, BF),
        jax.ShapeDtypeStruct((1,) + grid_shape, BF),
        jax.ShapeDtypeStruct((C, C), F32),
        jax.ShapeDtypeStruct((2, C, C, M * M), F32),
    )
    results = pl.pallas_call(
        step_kernel,
        in_specs=[anywhere] * 3 + [on_chip] + [anywhere] * len(tables),
        out_specs=(on_chip,) * 8,
        out_shape=(
            pltpu.VMEM((1,) + grid_shape, BF),
            pltpu.VMEM((ZL, 12, X, Y), BF),
            pltpu.VMEM((C, C), F32),
            pltpu.VMEM((2, C, C, M * M), F32),
            pltpu.VMEM(grid_shape, F32),
            planes,
            pltpu.VMEM(tables[-2].shape, BF),
            pltpu.VMEM(tables[-1].shape, BF),
        ),
        scratch_shapes=scratch,
        compiler_params=pltpu.CompilerParams(
            vmem_limit_bytes=VMEM_LIMIT, collective_id=0, has_side_effects=True
        ),
        name="step",
    )(fields, cotangent, spectral_weight, pointwise_weight, *tables)
    return pl.pallas_call(
        store_kernel,
        in_specs=[on_chip] * 8,
        out_specs=(anywhere,) * 4,
        out_shape=shapes,
        scratch_shapes=[
            pltpu.VMEM((4, 256, 256), F32),
            pltpu.VMEM((ZL, 4, X, Y), BF),
            pltpu.SemaphoreType.DMA((5,)),
        ],
        compiler_params=pltpu.CompilerParams(vmem_limit_bytes=8 * 1024 * 1024),
        name="store",
    )(*results)


def solution(mesh):
    placed = (
        P("dp", "gz", None, None, None),
        P("dp", "gz", None, None, None),
        P(None, None, None, "gz"),
        P(),
    )
    return jax.shard_map(
        shards,
        mesh=mesh,
        in_specs=placed,
        out_specs=(
            P("dp", "gz", None, None, None),
            P("dp", "gz", None, None, None),
            P(),
            P(None, None, None, "gz"),
        ),
        check_vma=False,
    )
```
